256 devices in a mesh: tm: 16 (over z, core), row: 16 (over x, y).
Axes of the slice: x: 4, y: 4, z: 8, core: 2. Of those that a mesh axis runs over, the one named last changes fastest.
Arguments:
- prior_ensemble: float32 [128, 128, 4096], P('tm', None, 'row'), may hold values from -6 to 6
- observation_data: float32 [128, 8192], P('tm', 'row'), may hold values from -24 to 24
- inverse_error_spread: float32 [8192], P('row'), may hold values from 0.024902152 to 0.24902152
- anomaly_inflation: float32 [128], P('tm'), may hold values from 1.1 to 1.4
- nonzero_tiles: float32 [64, 8, 128, 128], P('row'), may hold values from -0.1875 to 0.1875
- nonzero_tile_targets: int32 [64, 8], P('row'), may hold values from 0 to 31, as said below
Outputs:
- smoothed_ensemble: float32 [128, 128, 4096], P('tm', None, 'row')
- filtered_ensemble: float32 [128, 128, 4096], P('tm', None, 'row')
The draws below stay inside these ranges and needn't reach their ends.
Inputs may be any that keep to these rules, and one draw needn't show every extreme that they name: `nonzero_tile_targets`: in each block row the 8 block columns are distinct.
All inputs are finite; a program needn't handle non-finite values. Where the reference program divides by a largest or mean magnitude, that divisor is 1e-20 or more.
Results may differ from the reference program's by a relative error of at most 0.0003.
Values sent between devices are 32-bit elements; how exact they have to be, the bound alone decides.
A program may use at most 64 MiB of HBM per device.

```python
import math
import jax
import jax.numpy as jnp
from jax import lax

DIMENSION = 4096
NOBS = 8192
BLK = 128
NNZB = 8
ENSEMBLE_SIZE = 128
NS_ITERS = 8
HORIZON_LENGTH = 128
NBR = 64
NBC = 32


def draw_nonzero_tile_targets(key, part):
    row_keys = jax.random.split(key, NBR)
    picked = jax.vmap(lambda row_key: jax.random.permutation(row_key, NBC)[:NNZB])(row_keys)
    return picked.astype(jnp.int32)


def levels(key, dims, shards, least, high):
    gain, own = 1.0, jax.random.fold_in(key, 6)
    for dim, blocks in shards:
        steps = jnp.exp(jax.random.uniform(jax.random.fold_in(own, dim), (blocks,), jnp.float32, least / len(shards), high / len(shards)))
        gain = gain * jnp.repeat(steps, dims[dim] // blocks).reshape([-1 if axis == dim else 1 for axis in range(len(dims))])
    return gain


def noise(own_key, extent, width, bound, cuts=(), kind=jnp.bfloat16):
    array = jax.random.normal(own_key, extent, jnp.float32) * width
    if len(cuts) > 0:
        array = levels(own_key, extent, cuts, -0.22, 0.18) * array
    return jnp.clip(array, min=-bound, max=bound).astype(kind)


def setup_inputs(seed: int = 0) -> dict:
    splits = jax.random.split(jax.random.key(seed), 7)
    prior_ensemble = noise(splits[0], (HORIZON_LENGTH, ENSEMBLE_SIZE, DIMENSION), 1.0, 6.0, ((0, 16), (2, 16)), jnp.float32)
    observation_data = noise(splits[1], (HORIZON_LENGTH, NOBS), 4.0, 24.0, ((0, 16), (1, 16)), jnp.float32)
    inverse_error_spread = jnp.clip(jnp.exp(math.log(0.24902152) - 2.3025851 * jax.random.uniform(splits[2], (NOBS,), jnp.float32) ** levels(splits[2], (NOBS,), ((0, 16),), -0.2, 0.2)), 0.024902152, 0.24902152)
    anomaly_inflation = jnp.clip(1.1 + 0.29999995 * jax.random.uniform(splits[3], (HORIZON_LENGTH,), jnp.float32) ** levels(splits[3], (HORIZON_LENGTH,), ((0, 16),), -0.2, 0.2), 1.1, 1.4)
    nonzero_tiles = noise(splits[4], (NBR, NNZB, BLK, BLK), (NNZB * BLK) ** -0.5, 0.1875, ((0, 16),), jnp.float32)
    nonzero_tile_targets = draw_nonzero_tile_targets(jax.random.fold_in(splits[6], 71), 0)
    return dict(prior_ensemble=prior_ensemble, observation_data=observation_data, inverse_error_spread=inverse_error_spread, anomaly_inflation=anomaly_inflation, nonzero_tiles=nonzero_tiles, nonzero_tile_targets=nonzero_tile_targets)


exact_product = lax.Precision.HIGHEST

def ensemble_transforms(info_matrix, info_vector, anomaly_inflation):
    ensemble_entries = info_matrix.shape[-1]
    identity = jnp.eye(ensemble_entries, dtype=jnp.float32)
    row_bound = lax.optimization_barrier(jnp.max(lax.optimization_barrier(jnp.sum(jnp.abs(info_matrix), axis=2)), axis=1))
    scaled = info_matrix / row_bound[:, None, None]
    root_iter = scaled
    inv_iter = jnp.broadcast_to(identity, scaled.shape)
    for _ in range(NS_ITERS):
        update = 1.5 * identity - 0.5 * jnp.matmul(inv_iter, root_iter, precision=exact_product)
        root_iter = jnp.matmul(root_iter, update, precision=exact_product)
        inv_iter = jnp.matmul(update, inv_iter, precision=exact_product)
    inverse_root = inv_iter / jnp.sqrt(row_bound)[:, None, None]
    half_weights = jnp.einsum('tab,tb->ta', inverse_root, info_vector, precision=exact_product)
    mean_weights = jnp.einsum('tab,tb->ta', inverse_root, half_weights, precision=exact_product)
    spread_norm = float(ensemble_entries - 1) ** 0.5
    mixing = mean_weights[:, :, None] / spread_norm + anomaly_inflation[:, None, None] * inverse_root
    mixing = mixing - lax.optimization_barrier(jnp.mean(mixing, axis=1, keepdims=True))
    return mixing + 1.0 / ensemble_entries

def observe_ensemble(ensemble_vectors, nonzero_tiles, nonzero_tile_targets):
    ensemble_entries = ensemble_vectors.shape[0]
    blocks = ensemble_vectors.reshape(ensemble_entries, NBC, BLK)[:, nonzero_tile_targets]
    result = jnp.einsum('mbkj,bkij->mbi', blocks, nonzero_tiles, precision=exact_product)
    return result.reshape(ensemble_entries, NOBS)

def reference(prior_ensemble, observation_data, inverse_error_spread, anomaly_inflation, nonzero_tiles, nonzero_tile_targets):
    predicted_observations = lax.map(lambda ensemble_vectors: observe_ensemble(ensemble_vectors, nonzero_tiles, nonzero_tile_targets), prior_ensemble)
    obs_mean = lax.optimization_barrier(jnp.mean(predicted_observations, axis=1))
    whitened = (predicted_observations - obs_mean[:, None, :]) * inverse_error_spread / float(ENSEMBLE_SIZE - 1) ** 0.5
    innovation = (observation_data - obs_mean) * inverse_error_spread
    info_matrix = jnp.einsum('tmo,tno->tmn', whitened, whitened, precision=exact_product)
    info_matrix = info_matrix + jnp.eye(ENSEMBLE_SIZE, dtype=jnp.float32)
    info_vector = jnp.einsum('tmo,to->tm', whitened, innovation, precision=exact_product)
    ensemble_weight_factors = ensemble_transforms(info_matrix, info_vector, anomaly_inflation)
    filtered_ensemble = jnp.einsum('fjn,fjt->fnt', ensemble_weight_factors, prior_ensemble, precision=exact_product)

    def backward(running, transform):
        product = jnp.matmul(transform, running, precision=exact_product)
        return (product, product)
    _, suffix_product = lax.scan(backward, jnp.eye(ENSEMBLE_SIZE, dtype=jnp.float32), ensemble_weight_factors, reverse=True)
    smoothed_ensemble = jnp.einsum('fjn,fjt->fnt', suffix_product, prior_ensemble, precision=exact_product)
    return (smoothed_ensemble, filtered_ensemble)
```

```python
import functools

import jax
import jax.numpy as jnp
from jax import lax
from jax.experimental import pallas as pl
from jax.experimental.pallas import tpu as pltpu
from jax.sharding import PartitionSpec as P

MESH = pl.DeviceIdType.MESH
NS_ITERS = 8
F32, BF16 = jnp.float32, jnp.bfloat16
NT = (((1,), (1,)), ((), ()))


def halves(value):
    high = value.astype(BF16)
    low = (value - high.astype(F32)).astype(BF16)
    return high, low


def product(left, right):
    lh, ll = halves(left)
    rh, rl = halves(right)
    row = jnp.concatenate([rh, rl], axis=1)
    wide = jnp.dot(
        jnp.concatenate([lh, ll], axis=1),
        jnp.concatenate([row, row], axis=0),
        preferred_element_type=F32,
    )
    n = right.shape[1]
    return wide[:, :n] + wide[:, n:]


def assimilate(
    x_ref, tiles_ref, obs_ref, spread_ref, targets_ref, inflation_ref,
    u_ref, s_ref,
    xg, tg, obg, spg, tgg, tgs, xh, xl, acc, part, parts, vbuf, vin, rloc,
    send, recv, local_sem,
):
    tm, row = lax.axis_index("tm"), lax.axis_index("row")
    mx, my = lax.div(row, 4), lax.rem(row, 4)
    last_tm = lax.axis_size("tm") - 1
    counter = [0]

    def at(x, y):
        return (tm, lax.rem(x + 4, 4) * 4 + lax.rem(y + 4, 4))

    def remote(src, dst, device):
        i = counter[0]
        counter[0] += 1
        return pltpu.make_async_remote_copy(
            src_ref=src, dst_ref=dst, send_sem=send.at[i], recv_sem=recv.at[i],
            device_id=device, device_id_type=MESH,
        )

    barrier = pltpu.get_barrier_semaphore()
    for d in (1, 2, 3):
        for device in (at(mx + d, my), at(mx, my + d)):
            pl.semaphore_signal(barrier, inc=1, device_id=device, device_id_type=MESH)
    peers = 6
    for d in (1, 2, 4, 8):
        @pl.when(tm >= d)
        def _():
            pl.semaphore_signal(barrier, inc=1, device_id=(tm - d, row), device_id_type=MESH)

        @pl.when(tm + d <= last_tm)
        def _():
            pl.semaphore_signal(barrier, inc=1, device_id=(tm + d, row), device_id_type=MESH)

        peers = peers + jnp.where(tm >= d, 1, 0) + jnp.where(tm + d <= last_tm, 1, 0)
    pl.semaphore_wait(barrier, peers)

    core = lax.rem(tm, 2)
    other = (tm + 1 - 2 * core, row)
    sent = []

    def start(copy):
        copy.start()
        sent.append(copy)
        return copy

    own_x = x_ref.at[pl.ds(2 * mx, 2)]
    across = {}
    for d in (1, 3, 2):
        xd = lax.rem(mx + d, 4)
        across[d] = start(remote(x_ref.at[pl.ds(2 * xd, 2)], xg.at[d, 0], at(mx + d, my)))
    up, down, up2, down2 = {}, {}, {}, {}
    up[0] = start(remote(own_x, xg.at[0, 1], at(mx, my + 1)))
    down[0] = start(remote(own_x, xg.at[0, 3], at(mx, my - 1)))
    small = []
    for d in (1, 2, 3):
        xd = lax.rem(mx + d, 4)
        small.append(start(remote(obs_ref.at[pl.ds(2 * xd, 2)], obg.at[d], at(mx + d, my))))
        small.append(start(remote(spread_ref, spg.at[d], at(mx + d, my))))
        small.append(start(remote(targets_ref, tgg.at[d], at(mx + d, my))))
    first, second = 2 * core, 2 * core + 1
    right, left = {}, {}
    right[0] = start(remote(tiles_ref.at[first], tg.at[1, first], at(mx + 1, my)))
    left[0] = start(remote(tiles_ref.at[second], tg.at[3, second], at(mx - 1, my)))
    right[1] = start(remote(tiles_ref.at[second], tg.at[1, second], at(mx + 1, my)))
    left[1] = start(remote(tiles_ref.at[first], tg.at[3, first], at(mx - 1, my)))

    locals_ = [
        pltpu.make_async_copy(own_x, xg.at[0, 0], local_sem.at[0]),
        pltpu.make_async_copy(tiles_ref, tg.at[0], local_sem.at[1]),
        pltpu.make_async_copy(obs_ref.at[pl.ds(2 * mx, 2)], obg.at[0], local_sem.at[2]),
        pltpu.make_async_copy(spread_ref, spg.at[0], local_sem.at[3]),
        pltpu.make_async_copy(targets_ref, tgg.at[0], local_sem.at[4]),
    ]
    for copy in locals_:
        copy.start()

    def split_state(k, q):
        chunk = lax.rem(mx - k + 4, 4) * 4 + lax.rem(my - q + 4, 4)
        for t in (0, 1):
            for half in (0, 1):
                high, low = halves(xg[k, q, t, :, half * 128:(half + 1) * 128])
                xh[2 * chunk + half, t * 128:(t + 1) * 128, :] = high
                xl[2 * chunk + half, t * 128:(t + 1) * 128, :] = low

    for d in (1, 3, 2):
        across[d].wait_recv()
        up[d] = start(remote(xg.at[d, 0], xg.at[d, 1], at(mx, my + 1)))
        down[d] = start(remote(xg.at[d, 0], xg.at[d, 3], at(mx, my - 1)))
    for copy in locals_:
        copy.wait()
    for k in (0, 1, 3, 2):
        up[k].wait_recv()
        up2[k] = start(remote(xg.at[k, 1, 0], xg.at[k, 2, 0], at(mx, my + 1)))
        down[k].wait_recv()
        down2[k] = start(remote(xg.at[k, 3, 1], xg.at[k, 2, 1], at(mx, my - 1)))
        if k == 1:
            right[0].wait_recv()
            right2 = start(remote(tg.at[1, first], tg.at[2, first], at(mx + 1, my)))
            left[0].wait_recv()
            left2 = start(remote(tg.at[3, second], tg.at[2, second], at(mx - 1, my)))
        split_state(k, 0)
        split_state(k, 1)
        split_state(k, 3)
    passed = [
        start(remote(tg.at[1, first], tg.at[1, first], other)),
        start(remote(tg.at[3, second], tg.at[3, second], other)),
    ]
    right[1].wait_recv()
    passed.append(start(remote(tg.at[1, second], tg.at[1, second], other)))
    left[1].wait_recv()
    passed.append(start(remote(tg.at[3, first], tg.at[3, first], other)))
    for k in (0, 1, 3, 2):
        up2[k].wait_recv()
        down2[k].wait_recv()
        split_state(k, 2)
    right2.wait_recv()
    passed.append(start(remote(tg.at[2, first], tg.at[2, first], other)))
    left2.wait_recv()
    passed.append(start(remote(tg.at[2, second], tg.at[2, second], other)))
    for copy in small:
        copy.wait_recv()
    to_scalar = pltpu.make_async_copy(tgg, tgs, local_sem.at[0])
    to_scalar.start()
    to_scalar.wait()
    for copy in passed:
        copy.wait_recv()

    acc[...] = jnp.zeros_like(acc)

    def block_row(b, carry):
        k, i = lax.div(b, 4), lax.rem(b, 4)
        index = [tgs[k, i, j] for j in range(8)]
        th, tl = [], []
        for j in range(8):
            high, low = halves(tg[k, i, j])
            th.append(high)
            tl.append(low)
        th = jnp.concatenate(th, axis=1)
        tl = jnp.concatenate(tl, axis=1)
        high = jnp.concatenate([xh[j] for j in index], axis=1)
        low = jnp.concatenate([xl[j] for j in index], axis=1)
        wide = lax.dot_general(high, jnp.concatenate([th, tl], axis=0), NT, preferred_element_type=F32)
        obs = wide[:, :128] + wide[:, 128:]
        obs = obs + lax.dot_general(low, th, NT, preferred_element_type=F32)
        spread = spg[k, pl.ds(i, 1), :]
        for t in (0, 1):
            one = obs[t * 128:(t + 1) * 128, :]
            mean = jnp.sum(one, axis=0, keepdims=True) * (1.0 / 128.0)
            wh, wl = halves((one - mean) * (spread * (127.0 ** -0.5)))
            innovation = (obg[k, t, pl.ds(i, 1), :] - mean) * spread
            ih, il = halves(jnp.broadcast_to(innovation, (16, 128)))
            upper = lax.broadcasted_iota(jnp.int32, (16, 128), 0) < 8
            lines = jnp.where(upper, ih.astype(F32), il.astype(F32)).astype(BF16)
            acc[t] += lax.dot_general(
                jnp.concatenate([wh, lines], axis=0), jnp.concatenate([wh, wl], axis=0), NT,
                preferred_element_type=F32,
            )
        return carry

    lax.fori_loop(0, 16, block_row, 0)

    for t in (0, 1):
        cross = acc[t, 0:128, 128:256]
        part[t, 0:128, :] = acc[t, 0:128, 0:128] + cross + cross.T
        part[t, 128:136, :] = acc[t, 128:136, 0:128] + acc[t, 128:136, 128:256] + acc[t, 136:144, 0:128]
    sums = [start(remote(part, parts.at[d], at(mx, my + d))) for d in (1, 2, 3)]
    for copy in sums:
        copy.wait_recv()

    eye = (
        lax.broadcasted_iota(jnp.int32, (128, 128), 0) == lax.broadcasted_iota(jnp.int32, (128, 128), 1)
    ).astype(F32)
    state = []
    for t in (0, 1):
        total = part[t] + parts[1, t] + parts[2, t] + parts[3, t]
        info = total[0:128, :] + eye
        bound = jnp.max(jnp.sum(jnp.abs(info), axis=0, keepdims=True), axis=1, keepdims=True)
        m = info / bound
        state.append([m, 1.5 * eye - 0.5 * m, bound, total[128:136, :]])
    for _ in range(NS_ITERS - 1):
        for s in state:
            square = product(s[0], s[0])
            s[0] = product(s[0], 2.25 * eye - 1.5 * s[0] + 0.25 * square)
            s[1] = product(1.5 * eye - 0.5 * s[0], s[1])
    for t, (_, q, bound, vector) in enumerate(state):
        root = q / jnp.sqrt(bound)
        weights = product(product(vector, root), root)[0:1, :]
        mixing = weights * (127.0 ** -0.5) + inflation_ref[2 * mx + t] * root
        mixing = mixing - jnp.sum(mixing, axis=1, keepdims=True) * (1.0 / 128.0) + 1.0 / 128.0
        u_ref[2 * mx + t] = mixing
    mine = u_ref.at[pl.ds(2 * mx, 2)]
    shared = [start(remote(mine, mine, at(mx + d, my))) for d in (1, 2, 3)]
    for copy in shared:
        copy.wait_recv()

    u = [u_ref[t] for t in range(8)]
    p67, p45, p23, p01 = product(u[7], u[6]), product(u[5], u[4]), product(u[3], u[2]), product(u[1], u[0])
    p47 = product(p67, p45)
    p03 = product(p23, p01)
    p07 = product(p47, p03)
    running = p07
    vbuf[0] = running
    rloc[0] = p07
    rloc[4] = p47
    rloc[6] = p67
    rloc[7] = u[7]
    later = eye
    for level, d in enumerate((1, 2, 4, 8)):
        copy = remote(vbuf.at[level], vin.at[level], (tm - d, row))

        @pl.when(tm >= d)
        def _(copy=copy):
            copy.start()

        if level == 0:
            r5, r2 = product(p67, u[5]), product(p47, p23)
            rloc[5] = r5
            rloc[2] = r2
            rloc[3] = product(p47, u[3])
            rloc[1] = product(r2, u[1])

        @pl.when(tm + d <= last_tm)
        def _(copy=copy):
            copy.wait_recv()

        @pl.when(tm + d > last_tm)
        def _(level=level):
            vin[level] = eye

        got = vin[level]
        if level < 3:
            vbuf[level + 1] = product(got, vbuf[level])
        later = product(got, later)

        @pl.when(tm >= d)
        def _(copy=copy):
            copy.wait_send()

    for t in range(8):
        s_ref[t] = product(later, rloc[t])
    for copy in sent:
        copy.wait_send()


def apply(u_ref, s_ref, x_ref, smooth_ref, filter_ref):
    xh, xl = halves(x_ref[0])
    low = jnp.concatenate([xh, xl], axis=0)
    for m_ref, out_ref in ((s_ref, smooth_ref), (u_ref, filter_ref)):
        mh, ml = halves(m_ref[0])
        out_ref[0] = jnp.dot(jnp.concatenate([mh, mh], axis=1), low, preferred_element_type=F32) + jnp.dot(
            ml, xh, preferred_element_type=F32
        )


def local(prior, observations, spread, inflation, tiles, targets):
    obs = jnp.pad(observations.reshape(8, 4, 128), ((0, 0), (0, 4), (0, 0)))
    spr = jnp.pad(spread.reshape(4, 128), ((0, 4), (0, 0)))
    tgt = jnp.pad(targets, ((0, 4), (0, 120)))
    anywhere = pl.BlockSpec(memory_space=pl.ANY)
    vmem = pl.BlockSpec(memory_space=pltpu.VMEM)
    smem = pl.BlockSpec(memory_space=pltpu.SMEM)
    square = jax.ShapeDtypeStruct((8, 128, 128), F32)
    u, s = pl.pallas_call(
        assimilate,
        out_shape=(square, square),
        in_specs=[anywhere, anywhere, vmem, vmem, vmem, smem],
        out_specs=(vmem, vmem),
        scratch_shapes=[
            pltpu.VMEM((4, 4, 2, 128, 256), F32),
            pltpu.VMEM((4, 4, 8, 128, 128), F32),
            pltpu.VMEM((4, 2, 8, 128), F32),
            pltpu.VMEM((4, 8, 128), F32),
            pltpu.VMEM((4, 8, 128), jnp.int32),
            pltpu.SMEM((4, 8, 128), jnp.int32),
            pltpu.VMEM((32, 256, 128), BF16),
            pltpu.VMEM((32, 256, 128), BF16),
            pltpu.VMEM((2, 144, 256), F32),
            pltpu.VMEM((2, 136, 128), F32),
            pltpu.VMEM((4, 2, 136, 128), F32),
            pltpu.VMEM((4, 128, 128), F32),
            pltpu.VMEM((4, 128, 128), F32),
            pltpu.VMEM((8, 128, 128), F32),
            pltpu.SemaphoreType.DMA((64,)),
            pltpu.SemaphoreType.DMA((64,)),
            pltpu.SemaphoreType.DMA((5,)),
        ],
        compiler_params=pltpu.CompilerParams(
            collective_id=0, has_side_effects=True, vmem_limit_bytes=40 << 20
        ),
        name="assimilate",
    )(prior, tiles, obs, spr, tgt, inflation)
    step = lambda t: (t, 0, 0)
    whole = jax.ShapeDtypeStruct(prior.shape, F32)
    return pl.pallas_call(
        apply,
        grid=(8,),
        out_shape=(whole, whole),
        in_specs=[
            pl.BlockSpec((1, 128, 128), step),
            pl.BlockSpec((1, 128, 128), step),
            pl.BlockSpec((1, 128, 256), step),
        ],
        out_specs=(pl.BlockSpec((1, 128, 256), step), pl.BlockSpec((1, 128, 256), step)),
        name="apply",
    )(u, s, prior)


def solution(mesh):
    placed = (
        P("tm", None, "row"),
        P("tm", "row"),
        P("row"),
        P("tm"),
        P("row", None, None, None),
        P("row", None),
    )
    return jax.shard_map(
        local,
        mesh=mesh,
        in_specs=placed,
        out_specs=(P("tm", None, "row"), P("tm", None, "row")),
        check_vma=False,
    )
```

```python
import functools

import jax
import jax.numpy as jnp
from jax import lax
from jax.experimental import pallas as pl
from jax.experimental.pallas import tpu as pltpu
from jax.sharding import PartitionSpec as P

MESH = pl.DeviceIdType.MESH
NS_ITERS = 8
VMEM_LIMIT = 58 << 20
F32, BF16 = jnp.float32, jnp.bfloat16
NT = (((1,), (1,)), ((), ()))


def halves(value):
    high = value.astype(BF16)
    low = (value - high.astype(F32)).astype(BF16)
    return high, low


def product(left, right):
    lh, ll = halves(left)
    rh, rl = halves(right)
    row = jnp.concatenate([rh, rl], axis=1)
    wide = jnp.dot(
        jnp.concatenate([lh, ll], axis=1),
        jnp.concatenate([row, row], axis=0),
        preferred_element_type=F32,
    )
    n = right.shape[1]
    return wide[:, :n] + wide[:, n:]


PIECE = 192
SHARED = 16 * PIECE
STEPS, BLOCK_ROWS = 2, 16


def assimilate(
    x_ref, tiles_ref, obs_ref, spread_ref, targets_ref, inflation_ref,
    smooth_ref, filter_ref,
    xg, tg, xs, ts, xown, xah, xal, obg, spg, tgg, tgs, infl, acc, part, parts,
    u_ref, pbuf, vbuf, vin, rloc, yloc,
    send, recv, local_sem,
):
    tm, row = lax.axis_index("tm"), lax.axis_index("row")
    mx, my = lax.div(row, 4), lax.rem(row, 4)
    last_tm = 15
    counter = [0]

    def at(x, y):
        return (tm, lax.rem(x + 4, 4) * 4 + lax.rem(y + 4, 4))

    def along(d):
        return (lax.rem(tm + d + 16, 16), row)

    def remote(src, dst, device):
        i = counter[0]
        counter[0] += 1
        return pltpu.make_async_remote_copy(
            src_ref=src, dst_ref=dst, send_sem=send.at[i], recv_sem=recv.at[i],
            device_id=device, device_id_type=MESH,
        )

    own_x = lambda t: x_ref.at[2 * mx + t]
    own = [
        pltpu.make_async_copy(tiles_ref, tg.at[0], local_sem.at[0]),
        pltpu.make_async_copy(x_ref, xown, local_sem.at[1]),
        pltpu.make_async_copy(obs_ref, obg.at[0], local_sem.at[2]),
        pltpu.make_async_copy(spread_ref, spg.at[0], local_sem.at[3]),
        pltpu.make_async_copy(targets_ref, tgg.at[0], local_sem.at[4]),
        pltpu.make_async_copy(inflation_ref, infl, local_sem.at[5]),
        pltpu.make_async_copy(own_x(0), xg.at[0, 0, 0], local_sem.at[6]),
        pltpu.make_async_copy(own_x(1), xg.at[0, 0, 1], local_sem.at[7]),
    ]
    for copy in own:
        copy.start()

    barrier = pltpu.get_barrier_semaphore()
    near = [at(mx + d, my) for d in (1, 2, 3)] + [at(mx, my + d) for d in (1, 2, 3)]
    near += [along(d) for d in (1, -1, 2, -2, 4, -4, 8)]
    for device in near:
        pl.semaphore_signal(barrier, inc=1, device_id=device, device_id_type=MESH)
    pl.semaphore_wait(barrier, len(near))

    core = lax.rem(tm, 2)
    z = lax.div(tm, 2)
    other = (tm + 1 - 2 * core, row)
    sent = []

    def start(copy):
        copy.start()
        sent.append(copy)
        return copy

    across, up, down = {}, {}, {}

    def send_across(t):
        for d in (1, 3, 2):
            xd = lax.rem(mx + d, 4)
            across[t, d] = start(remote(x_ref.at[2 * xd + t], xg.at[d, 0, t], at(mx + d, my)))

    def send_y(t, k):
        src = own_x(t) if k == 0 else xg.at[k, 0, t]
        up[t, k] = start(remote(src, xg.at[k, 1, t], at(mx, my + 1)))
        down[t, k] = start(remote(src, xg.at[k, 3, t], at(mx, my - 1)))

    def send_y2(t):
        up[t, 4] = start(remote(xg.at[:, 1, t, 0:64], xg.at[:, 2, t, 0:64], at(mx, my + 1)))
        down[t, 4] = start(remote(xg.at[:, 3, t, 64:128], xg.at[:, 2, t, 64:128], at(mx, my - 1)))

    send_across(0)
    send_y(0, 0)
    piece = pl.ds(PIECE * tm, PIECE)
    brought = [start(remote(tiles_ref.at[piece], tg.at[d, piece], at(mx + d, my))) for d in (1, 3, 2)]
    send_across(1)
    rest = (4096 - SHARED) // 4
    first = pl.ds(SHARED + 2 * rest * core, rest)
    second = pl.ds(SHARED + 2 * rest * core + rest, rest)
    right = [start(remote(tiles_ref.at[first], tg.at[1, first], at(mx + 1, my)))]
    left = [start(remote(tiles_ref.at[second], tg.at[3, second], at(mx - 1, my)))]
    right.append(start(remote(tiles_ref.at[second], tg.at[1, second], at(mx + 1, my))))
    left.append(start(remote(tiles_ref.at[first], tg.at[3, first], at(mx - 1, my))))
    small = []
    for d in (1, 2, 3):
        small.append(start(remote(obs_ref, obg.at[d], at(mx + d, my))))
        small.append(start(remote(spread_ref, spg.at[d], at(mx + d, my))))
        small.append(start(remote(targets_ref, tgg.at[d], at(mx + d, my))))

    passed = []

    def unit(step, low=0, size=PIECE):
        at_z = lax.rem(z + step + 8, 8)
        return tg.at[pl.ds(1, 3), pl.ds(PIECE * (2 * at_z + core) + low, size)]

    def send_z(step):
        if step < 4:
            ahead = start(remote(unit(1 - step), unit(1 - step), along(2)))
            behind = start(remote(unit(step - 1), unit(step - 1), along(-2)))
        else:
            half = PIECE // 2
            ahead = start(remote(unit(-3, 0, half), unit(-3, 0, half), along(2)))
            behind = start(remote(unit(3, half, half), unit(3, half, half), along(-2)))
        return ahead, behind

    def pass_on(ref):
        passed.append(start(remote(ref, ref, other)))

    def split_state(t, k, q):
        chunk = lax.rem(mx - k + 4, 4) * 4 + lax.rem(my - q + 4, 4)
        for half in (0, 1):
            high, low = halves(xg[k, q, t, :, half * 128:(half + 1) * 128])
            xs[t, 2 * chunk + half, 0:128, :] = high
            xs[t, 2 * chunk + half, 128:256, :] = low

    def split_tiles(k):
        @pl.loop(0, 32)
        def _(n):
            high, low = halves(tg[k, pl.ds(pl.multiple_of(n * 128, 128), 128), :])
            ts[k * 32 + n, 0:128, :] = high
            ts[k * 32 + n, 128:256, :] = low

    def observe(t, k):
        for i in range(4):
            index = [tgs[k, i, j] for j in range(8)]
            state = jnp.concatenate([xs[t, j] for j in index], axis=1)
            block = jnp.concatenate([ts[(k * 4 + i) * 8 + j] for j in range(8)], axis=1)
            wide = lax.dot_general(state, block, NT, preferred_element_type=F32)
            one = (wide[0:128, 0:128] + wide[0:128, 128:256]) + (wide[128:256, 0:128] + wide[128:256, 128:256])
            spread = spg[k, i:i + 1, :]
            mean = jnp.sum(one, axis=0, keepdims=True) * (1.0 / 128.0)
            wh, wl = halves((one - mean) * (spread * (127.0 ** -0.5)))
            seen = jnp.where(chosen[t], obg[k, :, i * 128:(i + 1) * 128], 0.0)
            innovation = (jnp.sum(seen, axis=0, keepdims=True) - mean) * spread
            ih, il = halves(jnp.broadcast_to(innovation, (16, 128)))
            upper = lax.broadcasted_iota(jnp.int32, (16, 128), 0) < 8
            lines = jnp.where(upper, ih.astype(F32), il.astype(F32)).astype(BF16)
            acc[t] += lax.dot_general(
                jnp.concatenate([wh, lines], axis=0), jnp.concatenate([wh, wl], axis=0), NT,
                preferred_element_type=F32,
            )

    def reduce(t):
        cross = acc[t, 0:128, 128:256]
        part[t, 0:128, :] = acc[t, 0:128, 0:128] + cross + cross.T
        part[t, 128:136, :] = acc[t, 128:136, 0:128] + acc[t, 128:136, 128:256] + acc[t, 136:144, 0:128]
        return [start(remote(part.at[t], parts.at[d, t], at(mx, my + d))) for d in (1, 3, 2)]

    acc[...] = jnp.zeros_like(acc)
    chosen = [lax.broadcasted_iota(jnp.int32, (8, 128), 0) == 2 * mx + t for t in (0, 1)]
    for d in (1, 3, 2):
        across[0, d].wait_recv()
        send_y(0, d)
    for copy in brought:
        copy.wait_recv()
    steps = [send_z(1)]
    pass_on(unit(0))
    send_y(1, 0)
    for copy in own:
        copy.wait()
    split_tiles(0)
    for copy in steps[0]:
        copy.wait_recv()
    steps.append(send_z(2))
    pass_on(unit(-1))
    pass_on(unit(1))
    for k in (0, 1, 3, 2):
        up[0, k].wait_recv()
        down[0, k].wait_recv()
    send_y2(0)
    for d in (1, 3, 2):
        across[1, d].wait_recv()
        send_y(1, d)
    right[0].wait_recv()
    right2 = start(remote(tg.at[1, first], tg.at[2, first], at(mx + 1, my)))
    left[0].wait_recv()
    left2 = start(remote(tg.at[3, second], tg.at[2, second], at(mx - 1, my)))
    right[1].wait_recv()
    left[1].wait_recv()
    pass_on(tg.at[1, pl.ds(SHARED + 2 * rest * core, 2 * rest)])
    pass_on(tg.at[3, pl.ds(SHARED + 2 * rest * core, 2 * rest)])
    for copy in small:
        copy.wait_recv()
    to_scalar = pltpu.make_async_copy(tgg, tgs, local_sem.at[0])
    to_scalar.start()
    for k in range(4):
        split_state(0, k, 0)
        split_state(0, k, 1)
        split_state(0, k, 3)
    for copy in steps[1]:
        copy.wait_recv()
    steps.append(send_z(3))
    pass_on(unit(-2))
    pass_on(unit(2))
    for k in range(4):
        split_state(1, k, 0)
    for t in range(8):
        xah[t], xal[t] = halves(xown[t])
    up[0, 4].wait_recv()
    down[0, 4].wait_recv()
    for k in range(4):
        split_state(0, k, 2)
    to_scalar.wait()
    for copy in steps[2]:
        copy.wait_recv()
    steps.append(send_z(4))
    pass_on(unit(-3))
    pass_on(unit(3))
    observe(0, 0)
    right2.wait_recv()
    left2.wait_recv()
    pass_on(tg.at[2, pl.ds(SHARED + 2 * rest * core, 2 * rest)])
    for k in (0, 1, 3, 2):
        up[1, k].wait_recv()
        down[1, k].wait_recv()
    send_y2(1)
    for copy in steps[3]:
        copy.wait_recv()
    pass_on(unit(4))
    for k in range(4):
        split_state(1, k, 1)
        split_state(1, k, 3)
    for copy in passed:
        copy.wait_recv()
    for k in (1, 2, 3):
        split_tiles(k)
        observe(0, k)
    sums = reduce(0)
    up[1, 4].wait_recv()
    down[1, 4].wait_recv()
    for k in range(4):
        split_state(1, k, 2)
    for k in range(4):
        observe(1, k)
    sums += reduce(1)
    for copy in sums:
        copy.wait_recv()

    eye = (
        lax.broadcasted_iota(jnp.int32, (128, 128), 0) == lax.broadcasted_iota(jnp.int32, (128, 128), 1)
    ).astype(F32)
    state = []
    for t in (0, 1):
        total = part[t] + parts[1, t] + parts[2, t] + parts[3, t]
        info = total[0:128, :] + eye
        bound = jnp.max(jnp.sum(jnp.abs(info), axis=0, keepdims=True), axis=1, keepdims=True)
        m = info / bound
        state.append([m, 1.5 * eye - 0.5 * m, bound, total[128:136, :]])
    for _ in range(NS_ITERS - 1):
        for s in state:
            square = product(s[0], s[0])
            s[0] = product(s[0], 2.25 * eye - 1.5 * s[0] + 0.25 * square)
            s[1] = product(1.5 * eye - 0.5 * s[0], s[1])
    for t, (_, q, bound, vector) in enumerate(state):
        root = q / jnp.sqrt(bound)
        weights = product(product(vector, root), root)[0:1, :]
        mixing = weights * (127.0 ** -0.5) + infl[2 * mx + t] * root
        mixing = mixing - jnp.sum(mixing, axis=1, keepdims=True) * (1.0 / 128.0) + 1.0 / 128.0
        u_ref[2 * mx + t] = mixing
    pbuf[mx] = product(u_ref[2 * mx + 1], u_ref[2 * mx])
    pairs = [start(remote(pbuf.at[mx], pbuf.at[mx], at(mx + d, my))) for d in (1, 3, 2)]
    mine = u_ref.at[pl.ds(2 * mx, 2)]
    shared = [start(remote(mine, mine, at(mx + d, my))) for d in (1, 3, 2)]
    for copy in pairs:
        copy.wait_recv()

    p0, p1, p2, p3 = [pbuf[i] for i in range(4)]
    p23 = product(p3, p2)
    p03 = product(p23, product(p1, p0))
    vbuf[0] = p03
    rloc[0] = p03
    rloc[4] = p23
    rloc[6] = p3

    def applied(t):
        both = jnp.concatenate([u_ref[t], rloc[t]], axis=0)
        high, low = halves(both)
        out = jnp.dot(
            jnp.concatenate([high, low], axis=1), jnp.concatenate([xah[t], xah[t]], axis=0),
            preferred_element_type=F32,
        ) + jnp.dot(high, xal[t], preferred_element_type=F32)
        filter_ref[t] = out[0:128]
        yh, yl = halves(out[128:256])
        yloc[t, 0:128, :] = yh
        yloc[t, 128:256, :] = yl

    later = eye
    for level, d in enumerate((1, 2, 4, 8)):
        copy = remote(vbuf.at[level], vin.at[level], along(-d))

        @pl.when(tm >= d)
        def _(copy=copy):
            copy.start()

        if level == 0:
            for other_copy in shared:
                other_copy.wait_recv()
            r2 = product(p23, p1)
            rloc[2] = r2
            rloc[7] = u_ref[7]
            rloc[5] = product(p3, u_ref[5])
            rloc[3] = product(p23, u_ref[3])
            rloc[1] = product(r2, u_ref[1])
        applied(2 * level)
        applied(2 * level + 1)

        @pl.when(tm + d <= last_tm)
        def _(copy=copy):
            copy.wait_recv()

        @pl.when(tm + d > last_tm)
        def _(level=level):
            vin[level] = eye

        got = vin[level]
        if level < 3:
            vbuf[level + 1] = product(got, vbuf[level])
        later = product(got, later)

        @pl.when(tm >= d)
        def _(copy=copy):
            copy.wait_send()

    lh, ll = halves(later)
    wide = jnp.concatenate([lh, lh], axis=1)
    for t in range(8):
        smooth_ref[t] = jnp.dot(wide, yloc[t], preferred_element_type=F32) + jnp.dot(
            ll, yloc[t, 0:128, :], preferred_element_type=F32
        )
    for copy in sent:
        copy.wait_send()


def local(prior, observations, spread, inflation, tiles, targets):
    anywhere = pl.BlockSpec(memory_space=pl.ANY)
    vmem = pl.BlockSpec(memory_space=pltpu.VMEM)
    whole = jax.ShapeDtypeStruct(prior.shape, F32)
    return pl.pallas_call(
        assimilate,
        out_shape=(whole, whole),
        in_specs=[anywhere] * 6,
        out_specs=(vmem, vmem),
        scratch_shapes=[
            pltpu.VMEM((4, 4, 2, 128, 256), F32),
            pltpu.VMEM((4, 4096, 128), F32),
            pltpu.VMEM((2, 32, 256, 128), BF16),
            pltpu.VMEM((128, 256, 128), BF16),
            pltpu.VMEM((8, 128, 256), F32),
            pltpu.VMEM((8, 128, 256), BF16),
            pltpu.VMEM((8, 128, 256), BF16),
            pltpu.VMEM((4, 8, 512), F32),
            pltpu.VMEM((4, 4, 128), F32),
            pltpu.VMEM((4, 4, 8), jnp.int32),
            pltpu.SMEM((4, 4, 8), jnp.int32),
            pltpu.SMEM((8,), F32),
            pltpu.VMEM((2, 144, 256), F32),
            pltpu.VMEM((2, 136, 128), F32),
            pltpu.VMEM((4, 2, 136, 128), F32),
            pltpu.VMEM((8, 128, 128), F32),
            pltpu.VMEM((4, 128, 128), F32),
            pltpu.VMEM((4, 128, 128), F32),
            pltpu.VMEM((4, 128, 128), F32),
            pltpu.VMEM((8, 128, 128), F32),
            pltpu.VMEM((8, 256, 256), BF16),
            pltpu.SemaphoreType.DMA((96,)),
            pltpu.SemaphoreType.DMA((96,)),
            pltpu.SemaphoreType.DMA((8,)),
        ],
        compiler_params=pltpu.CompilerParams(
            collective_id=0, has_side_effects=True, vmem_limit_bytes=VMEM_LIMIT
        ),
        name="assimilate",
    )(prior, tiles.reshape(4096, 128), observations, spread.reshape(4, 128), targets, inflation)


def solution(mesh):
    placed = (
        P("tm", None, "row"),
        P("tm", "row"),
        P("row"),
        P("tm"),
        P("row", None, None, None),
        P("row", None),
    )
    return jax.shard_map(
        local,
        mesh=mesh,
        in_specs=placed,
        out_specs=(P("tm", None, "row"), P("tm", None, "row")),
        check_vma=False,
    )
```

```python
import functools

import jax
import jax.numpy as jnp
from jax import lax
from jax.experimental import pallas as pl
from jax.experimental.pallas import tpu as pltpu
from jax.sharding import PartitionSpec as P

MESH = pl.DeviceIdType.MESH
NS_ITERS = 8
VMEM_LIMIT = 58 << 20
F32, BF16 = jnp.float32, jnp.bfloat16
NT = (((1,), (1,)), ((), ()))


def halves(value):
    high = value.astype(BF16)
    low = (value - high.astype(F32)).astype(BF16)
    return high, low


def product(left, right):
    lh, ll = halves(left)
    rh, rl = halves(right)
    row = jnp.concatenate([rh, rl], axis=1)
    wide = jnp.dot(
        jnp.concatenate([lh, ll], axis=1),
        jnp.concatenate([row, row], axis=0),
        preferred_element_type=F32,
    )
    n = right.shape[1]
    return wide[:, :n] + wide[:, n:]


PIECE = 128
SHARED = 16 * PIECE
STEPS, BLOCK_ROWS = 2, 16


def assimilate(
    x_ref, tiles_ref, obs_ref, spread_ref, targets_ref, inflation_ref,
    filter_ref, y_ref, later_ref,
    xg, tg, xs, ts, xown, xah, xal, obg, spg, tgg, tgs, infl, acc, part, parts,
    u_ref, pbuf, pown, pother, cown, cin, rloc, yloc, floc,
    send, recv, local_sem, out_sem,
):
    tm, row = lax.axis_index("tm"), lax.axis_index("row")
    mx, my = lax.div(row, 4), lax.rem(row, 4)
    core = lax.rem(tm, 2)
    z = lax.div(tm, 2)
    other = (tm + 1 - 2 * core, row)
    counter = [0]

    def at(x, y):
        return (tm, lax.rem(x + 4, 4) * 4 + lax.rem(y + 4, 4))

    def along(d):
        return (lax.rem(tm + d + 16, 16), row)

    def remote(src, dst, device):
        i = counter[0]
        counter[0] += 1
        return pltpu.make_async_remote_copy(
            src_ref=src, dst_ref=dst, send_sem=send.at[i], recv_sem=recv.at[i],
            device_id=device, device_id_type=MESH,
        )

    own_x = lambda t: x_ref.at[2 * mx + t]
    own = [
        pltpu.make_async_copy(tiles_ref, tg.at[0], local_sem.at[0]),
        pltpu.make_async_copy(x_ref, xown, local_sem.at[1]),
        pltpu.make_async_copy(obs_ref, obg.at[0], local_sem.at[2]),
        pltpu.make_async_copy(spread_ref, spg.at[0], local_sem.at[3]),
        pltpu.make_async_copy(targets_ref, tgg.at[0], local_sem.at[4]),
        pltpu.make_async_copy(inflation_ref, infl, local_sem.at[5]),
        pltpu.make_async_copy(own_x(0), xg.at[0, 0, 0], local_sem.at[6]),
        pltpu.make_async_copy(own_x(1), xg.at[0, 0, 1], local_sem.at[7]),
    ]
    for copy in own:
        copy.start()

    eye = (
        lax.broadcasted_iota(jnp.int32, (128, 128), 0) == lax.broadcasted_iota(jnp.int32, (128, 128), 1)
    ).astype(F32)
    for d in range(7):
        cin[d] = eye
    barrier = pltpu.get_barrier_semaphore()
    near = [at(mx + d, my) for d in (1, 2, 3)] + [at(mx, my + d) for d in (1, 2, 3)]
    near += [other] + [along(2 * d) for d in range(1, 8)]
    for device in near:
        pl.semaphore_signal(barrier, inc=1, device_id=device, device_id_type=MESH)
    pl.semaphore_wait(barrier, len(near))

    sent = []

    def start(copy):
        copy.start()
        sent.append(copy)
        return copy

    across, up, down = {}, {}, {}

    def send_across(t):
        for d in (1, 3, 2):
            xd = lax.rem(mx + d, 4)
            across[t, d] = start(remote(x_ref.at[2 * xd + t], xg.at[d, 0, t], at(mx + d, my)))

    def send_y(t, k):
        src = own_x(t) if k == 0 else xg.at[k, 0, t]
        up[t, k] = start(remote(src, xg.at[k, 1, t], at(mx, my + 1)))
        down[t, k] = start(remote(src, xg.at[k, 3, t], at(mx, my - 1)))

    far = {}

    def pass_y(t, k):
        up[t, k].wait_recv()
        one = start(remote(xg.at[k, 1, t, 0:64], xg.at[k, 2, t, 0:64], at(mx, my + 1)))
        down[t, k].wait_recv()
        two = start(remote(xg.at[k, 3, t, 64:128], xg.at[k, 2, t, 64:128], at(mx, my - 1)))
        far[t, k] = (one, two)

    send_across(0)
    send_y(0, 0)
    send_y(1, 0)
    piece = pl.ds(PIECE * tm, PIECE)
    brought = [start(remote(tiles_ref.at[piece], tg.at[d, piece], at(mx + d, my))) for d in (1, 3, 2)]
    rest = (4096 - SHARED) // 4
    first = pl.ds(SHARED + 2 * rest * core, rest)
    second = pl.ds(SHARED + 2 * rest * core + rest, rest)

    passed = []

    def unit(step, low=0, size=PIECE):
        at_z = lax.rem(z + step + 8, 8)
        return tg.at[pl.ds(1, 3), pl.ds(PIECE * (2 * at_z + core) + low, size)]

    def send_z(step):
        if step < 4:
            ahead = start(remote(unit(1 - step), unit(1 - step), along(2)))
            behind = start(remote(unit(step - 1), unit(step - 1), along(-2)))
        else:
            half = PIECE // 2
            ahead = start(remote(unit(-3, 0, half), unit(-3, 0, half), along(2)))
            behind = start(remote(unit(3, half, half), unit(3, half, half), along(-2)))
        return ahead, behind

    def pass_on(ref):
        passed.append(start(remote(ref, ref, other)))

    def split_state(t, k, q):
        chunk = lax.rem(mx - k + 4, 4) * 4 + lax.rem(my - q + 4, 4)
        for half in (0, 1):
            high, low = halves(xg[k, q, t, :, half * 128:(half + 1) * 128])
            xs[t, 2 * chunk + half, 0:128, :] = high
            xs[t, 2 * chunk + half, 128:256, :] = low

    def split_tiles(k, low, high_end):
        @pl.loop(low, high_end)
        def _(n):
            high, low = halves(tg[k, pl.ds(pl.multiple_of(n * 128, 128), 128), :])
            ts[k * 32 + n, 0:128, :] = high
            ts[k * 32 + n, 128:256, :] = low

    def observe(t, k, rows=(0, 1, 2, 3)):
        for i in rows:
            index = [tgs[k, i, j] for j in range(8)]
            state = jnp.concatenate([xs[t, j] for j in index], axis=1)
            block = jnp.concatenate([ts[(k * 4 + i) * 8 + j] for j in range(8)], axis=1)
            wide = lax.dot_general(state, block, NT, preferred_element_type=F32)
            one = (wide[0:128, 0:128] + wide[0:128, 128:256]) + (wide[128:256, 0:128] + wide[128:256, 128:256])
            spread = spg[k, i:i + 1, :]
            mean = jnp.sum(one, axis=0, keepdims=True) * (1.0 / 128.0)
            wh, wl = halves((one - mean) * (spread * (127.0 ** -0.5)))
            seen = jnp.where(chosen[t], obg[k, :, i * 128:(i + 1) * 128], 0.0)
            innovation = (jnp.sum(seen, axis=0, keepdims=True) - mean) * spread
            ih, il = halves(jnp.broadcast_to(innovation, (16, 128)))
            upper = lax.broadcasted_iota(jnp.int32, (16, 128), 0) < 8
            lines = jnp.where(upper, ih.astype(F32), il.astype(F32)).astype(BF16)
            acc[t] += lax.dot_general(
                jnp.concatenate([wh, lines], axis=0), jnp.concatenate([wh, wl], axis=0), NT,
                preferred_element_type=F32,
            )

    def reduce(t):
        cross = acc[t, 0:128, 128:256]
        part[t, 0:128, :] = acc[t, 0:128, 0:128] + cross + cross.T
        part[t, 128:136, :] = acc[t, 128:136, 0:128] + acc[t, 128:136, 128:256] + acc[t, 136:144, 0:128]
        return [start(remote(part.at[t], parts.at[d, t], at(mx, my + d))) for d in (1, 3, 2)]

    acc[...] = jnp.zeros_like(acc)
    chosen = [lax.broadcasted_iota(jnp.int32, (8, 128), 0) == 2 * mx + t for t in (0, 1)]
    across[0, 1].wait_recv()
    send_y(0, 1)
    across[0, 3].wait_recv()
    send_y(0, 3)
    send_across(1)
    across[0, 2].wait_recv()
    send_y(0, 2)
    pass_y(0, 0)
    pass_y(1, 0)
    for copy in brought:
        copy.wait_recv()
    steps = [send_z(1)]
    pass_on(unit(0))
    right = [start(remote(tiles_ref.at[first], tg.at[1, first], at(mx + 1, my)))]
    left = [start(remote(tiles_ref.at[second], tg.at[3, second], at(mx - 1, my)))]
    small = []
    for d in (1, 2, 3):
        small.append(start(remote(obs_ref, obg.at[d], at(mx + d, my))))
        small.append(start(remote(spread_ref, spg.at[d], at(mx + d, my))))
        small.append(start(remote(targets_ref, tgg.at[d], at(mx + d, my))))
    for copy in own:
        copy.wait()
    split_tiles(0, 0, 32)
    pass_y(0, 1)
    pass_y(0, 3)
    for d in (1, 3, 2):
        across[1, d].wait_recv()
        send_y(1, d)
    right.append(start(remote(tiles_ref.at[second], tg.at[1, second], at(mx + 1, my))))
    left.append(start(remote(tiles_ref.at[first], tg.at[3, first], at(mx - 1, my))))
    pass_y(0, 2)
    for copy in steps[0]:
        copy.wait_recv()
    steps.append(send_z(2))
    pass_on(unit(-1))
    pass_on(unit(1))
    right[0].wait_recv()
    right2 = start(remote(tg.at[1, first], tg.at[2, first], at(mx + 1, my)))
    left[0].wait_recv()
    left2 = start(remote(tg.at[3, second], tg.at[2, second], at(mx - 1, my)))
    for copy in small:
        copy.wait_recv()
    to_scalar = pltpu.make_async_copy(tgg, tgs, local_sem.at[0])
    to_scalar.start()
    for k in range(4):
        split_state(0, k, 0)
        split_state(0, k, 1)
        split_state(0, k, 3)
    pass_y(1, 1)
    for copy in steps[1]:
        copy.wait_recv()
    steps.append(send_z(3))
    pass_on(unit(-2))
    pass_on(unit(2))
    for k in (0, 1, 3, 2):
        for copy in far[0, k]:
            copy.wait_recv()
        split_state(0, k, 2)
        split_state(1, k, 0)
    right[1].wait_recv()
    pass_on(tg.at[1, pl.ds(SHARED + 2 * rest * core, 2 * rest)])
    left[1].wait_recv()
    pass_on(tg.at[3, pl.ds(SHARED + 2 * rest * core, 2 * rest)])
    pass_y(1, 3)
    to_scalar.wait()
    observe(0, 0, (0, 1))
    pass_y(1, 2)
    for copy in steps[2]:
        copy.wait_recv()
    steps.append(send_z(4))
    pass_on(unit(-3))
    pass_on(unit(3))
    right2.wait_recv()
    left2.wait_recv()
    pass_on(tg.at[2, pl.ds(SHARED + 2 * rest * core, 2 * rest)])
    observe(0, 0, (2, 3))
    for t in range(8):
        xah[t], xal[t] = halves(xown[t])
    for k in range(4):
        split_state(1, k, 1)
        split_state(1, k, 3)
    passed[5].wait_recv()
    passed[6].wait_recv()
    passed[9].wait_recv()
    shared_tiles = SHARED // 128
    for k in (1, 3):
        split_tiles(k, shared_tiles, 32)
        observe(0, k, (2, 3))
    for copy in steps[3]:
        copy.wait_recv()
    pass_on(unit(4))
    split_tiles(2, shared_tiles, 32)
    observe(0, 2, (2, 3))
    for i, copy in enumerate(passed):
        if i not in (5, 6, 9):
            copy.wait_recv()
    for k in (1, 2, 3):
        split_tiles(k, 0, shared_tiles)
        observe(0, k, (0, 1))
    sums = reduce(0)
    for k in (0, 1, 3, 2):
        for copy in far[1, k]:
            copy.wait_recv()
    for k in range(4):
        split_state(1, k, 2)
    for k in range(4):
        observe(1, k)
    sums += reduce(1)
    for copy in sums:
        copy.wait_recv()

    state = []
    for t in (0, 1):
        total = part[t] + parts[1, t] + parts[2, t] + parts[3, t]
        info = total[0:128, :] + eye
        bound = jnp.max(jnp.sum(jnp.abs(info), axis=0, keepdims=True), axis=1, keepdims=True)
        m = info / bound
        state.append([m, 1.5 * eye - 0.5 * m, bound, total[128:136, :]])
    for _ in range(NS_ITERS - 1):
        for s in state:
            square = product(s[0], s[0])
            s[0] = product(s[0], 2.25 * eye - 1.5 * s[0] + 0.25 * square)
            s[1] = product(1.5 * eye - 0.5 * s[0], s[1])
    for t, (_, q, bound, vector) in enumerate(state):
        root = q / jnp.sqrt(bound)
        weights = product(product(vector, root), root)[0:1, :]
        mixing = weights * (127.0 ** -0.5) + infl[2 * mx + t] * root
        mixing = mixing - jnp.sum(mixing, axis=1, keepdims=True) * (1.0 / 128.0) + 1.0 / 128.0
        u_ref[2 * mx + t] = mixing
    pbuf[mx] = product(u_ref[2 * mx + 1], u_ref[2 * mx])
    pairs = [start(remote(pbuf.at[mx], pbuf.at[mx], at(mx + d, my))) for d in (1, 3, 2)]
    mine = u_ref.at[pl.ds(2 * mx, 2)]
    shared = [start(remote(mine, mine, at(mx + d, my))) for d in (1, 3, 2)]
    for copy in pairs:
        copy.wait_recv()

    p0, p1, p2, p3 = [pbuf[i] for i in range(4)]
    p23 = product(p3, p2)
    p03 = product(p23, product(p1, p0))
    pown[...] = p03
    swap = start(remote(pown, pother, other))
    rloc[0] = p03
    rloc[4] = p23
    rloc[6] = p3
    swap.wait_recv()
    theirs = pother[...]
    odd = core == 1
    cown[...] = product(jnp.where(odd, p03, theirs), jnp.where(odd, theirs, p03))
    half_rows = pl.ds(64 * core, 64)
    down_z = []
    for d in range(1, 8):
        copy = remote(cown.at[half_rows], cin.at[d - 1, half_rows], along(-2 * d))
        down_z.append(copy)

        @pl.when(z >= d)
        def _(copy=copy):
            copy.start()

    for copy in shared:
        copy.wait_recv()
    r2 = product(p23, p1)
    rloc[2] = r2
    rloc[7] = u_ref[7]
    rloc[5] = product(p3, u_ref[5])
    rloc[3] = product(p23, u_ref[3])
    rloc[1] = product(r2, u_ref[1])
    stored = []
    for t in range(8):
        both = jnp.concatenate([u_ref[t], rloc[t]], axis=0)
        high, low = halves(both)
        out = jnp.dot(
            jnp.concatenate([high, low], axis=1), jnp.concatenate([xah[t], xah[t]], axis=0),
            preferred_element_type=F32,
        ) + jnp.dot(high, xal[t], preferred_element_type=F32)
        floc[t] = out[0:128]
        yh, yl = halves(out[128:256])
        yloc[t, 0:128, :] = yh
        yloc[t, 128:256, :] = yl
        for i, (src, dst) in enumerate(((floc, filter_ref), (yloc, y_ref))):
            stored.append(pltpu.make_async_copy(src.at[t], dst.at[t], out_sem.at[i, t]))
            stored[-1].start()

    for d in range(1, 8):
        @pl.when(z + d <= 7)
        def _(copy=down_z[d - 1]):
            copy.wait_recv()

    halves_swap = start(remote(cin.at[:, half_rows], cin.at[:, half_rows], other))
    halves_swap.wait_recv()
    c = [cin[d] for d in range(7)]
    upper = product(product(c[6], c[5]), product(c[4], c[3]))
    later = product(upper, product(product(c[2], c[1]), c[0]))
    later_ref[...] = jnp.where(odd, later, product(later, theirs))
    for copy in stored:
        copy.wait()
    for d in range(1, 8):
        @pl.when(z >= d)
        def _(copy=down_z[d - 1]):
            copy.wait_send()

    for copy in sent:
        copy.wait_send()


def smooth(later_ref, y_hbm, filter_hbm, smooth_out, filter_out, y, f, out, sem):
    f_in = pltpu.make_async_copy(filter_hbm, f, sem.at[16])
    f_out = pltpu.make_async_copy(f, filter_out, sem.at[17])
    y_in = [pltpu.make_async_copy(y_hbm.at[t], y.at[t], sem.at[t]) for t in range(8)]
    out_t = [pltpu.make_async_copy(out.at[t], smooth_out.at[t], sem.at[8 + t]) for t in range(8)]
    for copy in y_in:
        copy.start()
    f_in.start()
    high, low = halves(later_ref[...])
    wide = jnp.concatenate([high, high], axis=1)
    for t in range(8):
        y_in[t].wait()
        out[t] = jnp.dot(wide, y[t], preferred_element_type=F32) + jnp.dot(
            low, y[t, 0:128, :], preferred_element_type=F32
        )
        out_t[t].start()
        if t == 3:
            f_in.wait()
            f_out.start()
    f_out.wait()
    for copy in out_t:
        copy.wait()


def local(prior, observations, spread, inflation, tiles, targets):
    anywhere = pl.BlockSpec(memory_space=pl.ANY)
    vmem = pl.BlockSpec(memory_space=pltpu.VMEM)
    whole = jax.ShapeDtypeStruct(prior.shape, F32)
    filtered, y, later = pl.pallas_call(
        assimilate,
        out_shape=(whole, jax.ShapeDtypeStruct((8, 256, 256), BF16), jax.ShapeDtypeStruct((128, 128), F32)),
        in_specs=[anywhere] * 6,
        out_specs=(anywhere, anywhere, vmem),
        scratch_shapes=[
            pltpu.VMEM((4, 4, 2, 128, 256), F32),
            pltpu.VMEM((4, 4096, 128), F32),
            pltpu.VMEM((2, 32, 256, 128), BF16),
            pltpu.VMEM((128, 256, 128), BF16),
            pltpu.VMEM((8, 128, 256), F32),
            pltpu.VMEM((8, 128, 256), BF16),
            pltpu.VMEM((8, 128, 256), BF16),
            pltpu.VMEM((4, 8, 512), F32),
            pltpu.VMEM((4, 4, 128), F32),
            pltpu.VMEM((4, 4, 8), jnp.int32),
            pltpu.SMEM((4, 4, 8), jnp.int32),
            pltpu.SMEM((8,), F32),
            pltpu.VMEM((2, 144, 256), F32),
            pltpu.VMEM((2, 136, 128), F32),
            pltpu.VMEM((4, 2, 136, 128), F32),
            pltpu.VMEM((8, 128, 128), F32),
            pltpu.VMEM((4, 128, 128), F32),
            pltpu.VMEM((128, 128), F32),
            pltpu.VMEM((128, 128), F32),
            pltpu.VMEM((128, 128), F32),
            pltpu.VMEM((7, 128, 128), F32),
            pltpu.VMEM((8, 128, 128), F32),
            pltpu.VMEM((8, 256, 256), BF16),
            pltpu.VMEM((8, 128, 256), F32),
            pltpu.SemaphoreType.DMA((112,)),
            pltpu.SemaphoreType.DMA((112,)),
            pltpu.SemaphoreType.DMA((8,)),
            pltpu.SemaphoreType.DMA((2, 8)),
        ],
        compiler_params=pltpu.CompilerParams(
            collective_id=0, has_side_effects=True, vmem_limit_bytes=VMEM_LIMIT
        ),
        name="assimilate",
    )(prior, tiles.reshape(4096, 128), observations, spread.reshape(4, 128), targets, inflation)
    return pl.pallas_call(
        smooth,
        out_shape=(whole, whole),
        in_specs=[vmem, anywhere, anywhere],
        out_specs=(anywhere, anywhere),
        scratch_shapes=[
            pltpu.VMEM((8, 256, 256), BF16),
            pltpu.VMEM((8, 128, 256), F32),
            pltpu.VMEM((8, 128, 256), F32),
            pltpu.SemaphoreType.DMA((18,)),
        ],
        compiler_params=pltpu.CompilerParams(vmem_limit_bytes=VMEM_LIMIT),
        name="smooth",
    )(later, y, filtered)


def solution(mesh):
    placed = (
        P("tm", None, "row"),
        P("tm", "row"),
        P("row"),
        P("tm"),
        P("row", None, None, None),
        P("row", None),
    )
    return jax.shard_map(
        local,
        mesh=mesh,
        in_specs=placed,
        out_specs=(P("tm", None, "row"), P("tm", None, "row")),
        check_vma=False,
    )
```

```python
import functools

import jax
import jax.numpy as jnp
from jax import lax
from jax.experimental import pallas as pl
from jax.experimental.pallas import tpu as pltpu
from jax.sharding import PartitionSpec as P

MESH = pl.DeviceIdType.MESH
NS_ITERS = 8
VMEM_LIMIT = 40 << 20
F32, BF16 = jnp.float32, jnp.bfloat16
NT = (((1,), (1,)), ((), ()))


def halves(value):
    high = value.astype(BF16)
    low = (value - high.astype(F32)).astype(BF16)
    return high, low


def product(left, right):
    lh, ll = halves(left)
    rh, rl = halves(right)
    row = jnp.concatenate([rh, rl], axis=1)
    wide = jnp.dot(
        jnp.concatenate([lh, ll], axis=1),
        jnp.concatenate([row, row], axis=0),
        preferred_element_type=F32,
    )
    n = right.shape[1]
    return wide[:, :n] + wide[:, n:]


PIECE = 128
SHARED = 16 * PIECE
STEPS, BLOCK_ROWS = 2, 16


def assimilate(
    x_ref, tiles_ref, obs_ref, spread_ref, targets_ref, inflation_ref,
    filter_ref, y_ref, later_ref,
    xg, tg, xs, ts, xown, xah, xal, obg, spg, tgg, tgs, infl, acc, part, parts,
    u_ref, pbuf, pown, pother, cown, cin, rloc,
    send, recv, local_sem,
):
    tm, row = lax.axis_index("tm"), lax.axis_index("row")
    mx, my = lax.div(row, 4), lax.rem(row, 4)
    core = lax.rem(tm, 2)
    z = lax.div(tm, 2)
    other = (tm + 1 - 2 * core, row)
    counter = [0]

    def at(x, y):
        return (tm, lax.rem(x + 4, 4) * 4 + lax.rem(y + 4, 4))

    def along(d):
        return (lax.rem(tm + d + 16, 16), row)

    def remote(src, dst, device):
        i = counter[0]
        counter[0] += 1
        return pltpu.make_async_remote_copy(
            src_ref=src, dst_ref=dst, send_sem=send.at[i], recv_sem=recv.at[i],
            device_id=device, device_id_type=MESH,
        )

    own_x = lambda t: x_ref.at[2 * mx + t]
    own = [
        pltpu.make_async_copy(tiles_ref, tg.at[0], local_sem.at[0]),
        pltpu.make_async_copy(x_ref, xown, local_sem.at[1]),
        pltpu.make_async_copy(obs_ref, obg.at[0], local_sem.at[2]),
        pltpu.make_async_copy(spread_ref, spg.at[0], local_sem.at[3]),
        pltpu.make_async_copy(targets_ref, tgg.at[0], local_sem.at[4]),
        pltpu.make_async_copy(inflation_ref, infl, local_sem.at[5]),
        pltpu.make_async_copy(own_x(0), xg.at[0, 0, 0], local_sem.at[6]),
        pltpu.make_async_copy(own_x(1), xg.at[0, 0, 1], local_sem.at[7]),
    ]
    for copy in own:
        copy.start()

    eye = (
        lax.broadcasted_iota(jnp.int32, (128, 128), 0) == lax.broadcasted_iota(jnp.int32, (128, 128), 1)
    ).astype(F32)
    for d in range(7):
        cin[d] = eye
    barrier = pltpu.get_barrier_semaphore()
    near = [at(mx + d, my) for d in (1, 2, 3)] + [at(mx, my + d) for d in (1, 2, 3)]
    near += [other] + [along(2 * d) for d in range(1, 8)]
    for device in near:
        pl.semaphore_signal(barrier, inc=1, device_id=device, device_id_type=MESH)
    pl.semaphore_wait(barrier, len(near))

    sent = []

    def start(copy):
        copy.start()
        sent.append(copy)
        return copy

    across, up, down = {}, {}, {}

    def send_across(t):
        for d in (1, 3, 2):
            xd = lax.rem(mx + d, 4)
            across[t, d] = start(remote(x_ref.at[2 * xd + t], xg.at[d, 0, t], at(mx + d, my)))

    def send_y(t, k):
        src = own_x(t) if k == 0 else xg.at[k, 0, t]
        up[t, k] = start(remote(src, xg.at[k, 1, t], at(mx, my + 1)))
        down[t, k] = start(remote(src, xg.at[k, 3, t], at(mx, my - 1)))

    far = {}

    def pass_y(t, k):
        up[t, k].wait_recv()
        one = start(remote(xg.at[k, 1, t, 0:64], xg.at[k, 2, t, 0:64], at(mx, my + 1)))
        down[t, k].wait_recv()
        two = start(remote(xg.at[k, 3, t, 64:128], xg.at[k, 2, t, 64:128], at(mx, my - 1)))
        far[t, k] = (one, two)

    send_across(0)
    send_y(0, 0)
    send_y(1, 0)
    piece = pl.ds(PIECE * tm, PIECE)
    brought = [start(remote(tiles_ref.at[piece], tg.at[d, piece], at(mx + d, my))) for d in (1, 3, 2)]
    rest = (4096 - SHARED) // 4
    first = pl.ds(SHARED + 2 * rest * core, rest)
    second = pl.ds(SHARED + 2 * rest * core + rest, rest)

    passed = []

    def unit(step, low=0, size=PIECE):
        at_z = lax.rem(z + step + 8, 8)
        return tg.at[pl.ds(1, 3), pl.ds(PIECE * (2 * at_z + core) + low, size)]

    def send_z(step):
        if step < 4:
            ahead = start(remote(unit(1 - step), unit(1 - step), along(2)))
            behind = start(remote(unit(step - 1), unit(step - 1), along(-2)))
        else:
            half = PIECE // 2
            ahead = start(remote(unit(-3, 0, half), unit(-3, 0, half), along(2)))
            behind = start(remote(unit(3, half, half), unit(3, half, half), along(-2)))
        return ahead, behind

    def pass_on(ref):
        passed.append(start(remote(ref, ref, other)))

    def split_state(t, k, q):
        chunk = lax.rem(mx - k + 4, 4) * 4 + lax.rem(my - q + 4, 4)
        for half in (0, 1):
            high, low = halves(xg[k, q, t, :, half * 128:(half + 1) * 128])
            xs[t, 2 * chunk + half, 0:128, :] = high
            xs[t, 2 * chunk + half, 128:256, :] = low

    def split_tiles(k, low, high_end):
        @pl.loop(low, high_end)
        def _(n):
            high, low = halves(tg[k, pl.ds(pl.multiple_of(n * 128, 128), 128), :])
            ts[k * 32 + n, 0:128, :] = high
            ts[k * 32 + n, 128:256, :] = low

    def observe(t, k, rows=(0, 1, 2, 3)):
        for i in rows:
            index = [tgs[k, i, j] for j in range(8)]
            state = jnp.concatenate([xs[t, j] for j in index], axis=1)
            block = jnp.concatenate([ts[(k * 4 + i) * 8 + j] for j in range(8)], axis=1)
            wide = lax.dot_general(state, block, NT, preferred_element_type=F32)
            one = (wide[0:128, 0:128] + wide[0:128, 128:256]) + (wide[128:256, 0:128] + wide[128:256, 128:256])
            spread = spg[k, i:i + 1, :]
            mean = jnp.sum(one, axis=0, keepdims=True) * (1.0 / 128.0)
            wh, wl = halves((one - mean) * (spread * (127.0 ** -0.5)))
            seen = jnp.where(chosen[t], obg[k, :, i * 128:(i + 1) * 128], 0.0)
            innovation = (jnp.sum(seen, axis=0, keepdims=True) - mean) * spread
            ih, il = halves(jnp.broadcast_to(innovation, (16, 128)))
            upper = lax.broadcasted_iota(jnp.int32, (16, 128), 0) < 8
            lines = jnp.where(upper, ih.astype(F32), il.astype(F32)).astype(BF16)
            acc[t] += lax.dot_general(
                jnp.concatenate([wh, lines], axis=0), jnp.concatenate([wh, wl], axis=0), NT,
                preferred_element_type=F32,
            )

    def reduce(t):
        cross = acc[t, 0:128, 128:256]
        part[t, 0:128, :] = acc[t, 0:128, 0:128] + cross + cross.T
        part[t, 128:136, :] = acc[t, 128:136, 0:128] + acc[t, 128:136, 128:256] + acc[t, 136:144, 0:128]
        return [start(remote(part.at[t], parts.at[d, t], at(mx, my + d))) for d in (1, 3, 2)]

    acc[...] = jnp.zeros_like(acc)
    chosen = [lax.broadcasted_iota(jnp.int32, (8, 128), 0) == 2 * mx + t for t in (0, 1)]
    across[0, 1].wait_recv()
    send_y(0, 1)
    across[0, 3].wait_recv()
    send_y(0, 3)
    send_across(1)
    across[0, 2].wait_recv()
    send_y(0, 2)
    pass_y(0, 0)
    pass_y(1, 0)
    for copy in brought:
        copy.wait_recv()
    steps = [send_z(1)]
    pass_on(unit(0))
    right = [start(remote(tiles_ref.at[first], tg.at[1, first], at(mx + 1, my)))]
    left = [start(remote(tiles_ref.at[second], tg.at[3, second], at(mx - 1, my)))]
    small = []
    for d in (1, 2, 3):
        small.append(start(remote(obs_ref, obg.at[d], at(mx + d, my))))
        small.append(start(remote(spread_ref, spg.at[d], at(mx + d, my))))
        small.append(start(remote(targets_ref, tgg.at[d], at(mx + d, my))))
    for copy in own:
        copy.wait()
    split_tiles(0, 0, 32)
    pass_y(0, 1)
    pass_y(0, 3)
    for d in (1, 3, 2):
        across[1, d].wait_recv()
        send_y(1, d)
    right.append(start(remote(tiles_ref.at[second], tg.at[1, second], at(mx + 1, my))))
    left.append(start(remote(tiles_ref.at[first], tg.at[3, first], at(mx - 1, my))))
    pass_y(0, 2)
    for copy in steps[0]:
        copy.wait_recv()
    steps.append(send_z(2))
    pass_on(unit(-1))
    pass_on(unit(1))
    right[0].wait_recv()
    right2 = start(remote(tg.at[1, first], tg.at[2, first], at(mx + 1, my)))
    left[0].wait_recv()
    left2 = start(remote(tg.at[3, second], tg.at[2, second], at(mx - 1, my)))
    for copy in small:
        copy.wait_recv()
    to_scalar = pltpu.make_async_copy(tgg, tgs, local_sem.at[0])
    to_scalar.start()
    for k in range(4):
        split_state(0, k, 0)
        split_state(0, k, 1)
        split_state(0, k, 3)
    pass_y(1, 1)
    for copy in steps[1]:
        copy.wait_recv()
    steps.append(send_z(3))
    pass_on(unit(-2))
    pass_on(unit(2))
    for k in (0, 1, 3, 2):
        for copy in far[0, k]:
            copy.wait_recv()
        split_state(0, k, 2)
        split_state(1, k, 0)
    right[1].wait_recv()
    pass_on(tg.at[1, pl.ds(SHARED + 2 * rest * core, 2 * rest)])
    left[1].wait_recv()
    pass_on(tg.at[3, pl.ds(SHARED + 2 * rest * core, 2 * rest)])
    pass_y(1, 3)
    to_scalar.wait()
    observe(0, 0, (0, 1))
    pass_y(1, 2)
    for copy in steps[2]:
        copy.wait_recv()
    steps.append(send_z(4))
    pass_on(unit(-3))
    pass_on(unit(3))
    right2.wait_recv()
    left2.wait_recv()
    pass_on(tg.at[2, pl.ds(SHARED + 2 * rest * core, 2 * rest)])
    observe(0, 0, (2, 3))
    for t in range(8):
        xah[t], xal[t] = halves(xown[t])
    for k in range(4):
        split_state(1, k, 1)
        split_state(1, k, 3)
    passed[5].wait_recv()
    passed[6].wait_recv()
    passed[9].wait_recv()
    shared_tiles = SHARED // 128
    for k in (1, 3):
        split_tiles(k, shared_tiles, 32)
        observe(0, k, (2, 3))
    for copy in steps[3]:
        copy.wait_recv()
    pass_on(unit(4))
    split_tiles(2, shared_tiles, 32)
    observe(0, 2, (2, 3))
    for i, copy in enumerate(passed):
        if i not in (5, 6, 9):
            copy.wait_recv()
    for k in (1, 2, 3):
        split_tiles(k, 0, shared_tiles)
        observe(0, k, (0, 1))
    sums = reduce(0)
    for k in (0, 1, 3, 2):
        for copy in far[1, k]:
            copy.wait_recv()
    for k in range(4):
        split_state(1, k, 2)
    for k in range(4):
        observe(1, k)
    sums += reduce(1)
    for copy in sums:
        copy.wait_recv()

    state = []
    for t in (0, 1):
        total = part[t] + parts[1, t] + parts[2, t] + parts[3, t]
        info = total[0:128, :] + eye
        bound = jnp.max(jnp.sum(jnp.abs(info), axis=0, keepdims=True), axis=1, keepdims=True)
        m = info / bound
        state.append([m, 1.5 * eye - 0.5 * m, bound, total[128:136, :]])
    for _ in range(NS_ITERS - 1):
        for s in state:
            square = product(s[0], s[0])
            s[0] = product(s[0], 2.25 * eye - 1.5 * s[0] + 0.25 * square)
            s[1] = product(1.5 * eye - 0.5 * s[0], s[1])
    for t, (_, q, bound, vector) in enumerate(state):
        root = q / jnp.sqrt(bound)
        weights = product(product(vector, root), root)[0:1, :]
        mixing = weights * (127.0 ** -0.5) + infl[2 * mx + t] * root
        mixing = mixing - jnp.sum(mixing, axis=1, keepdims=True) * (1.0 / 128.0) + 1.0 / 128.0
        u_ref[2 * mx + t] = mixing
    pbuf[mx] = product(u_ref[2 * mx + 1], u_ref[2 * mx])
    pairs = [start(remote(pbuf.at[mx], pbuf.at[mx], at(mx + d, my))) for d in (1, 3, 2)]
    for copy in pairs:
        copy.wait_recv()
    mine = u_ref.at[pl.ds(2 * mx, 2)]
    shared = [start(remote(mine, mine, at(mx + d, my))) for d in (1, 3, 2)]

    p0, p1, p2, p3 = [pbuf[i] for i in range(4)]
    p23 = product(p3, p2)
    p03 = product(p23, product(p1, p0))
    pown[...] = p03
    swap = start(remote(pown, pother, other))
    rloc[0] = p03
    rloc[4] = p23
    rloc[6] = p3
    swap.wait_recv()
    theirs = pother[...]
    odd = core == 1
    cown[...] = product(jnp.where(odd, p03, theirs), jnp.where(odd, theirs, p03))
    half_rows = pl.ds(64 * core, 64)
    down_z = {}
    for d in (4, 3, 5, 2, 6, 1, 7):
        copy = remote(cown.at[half_rows], cin.at[d - 1, half_rows], along(-2 * d))
        down_z[d] = copy

        @pl.when(z >= d)
        def _(copy=copy):
            copy.start()

    for copy in shared:
        copy.wait_recv()
    r2 = product(p23, p1)
    rloc[2] = r2
    rloc[7] = u_ref[7]
    rloc[5] = product(p3, u_ref[5])
    rloc[3] = product(p23, u_ref[3])
    rloc[1] = product(r2, u_ref[1])
    for t in range(8):
        both = jnp.concatenate([u_ref[t], rloc[t]], axis=0)
        high, low = halves(both)
        out = jnp.dot(
            jnp.concatenate([high, low], axis=1), jnp.concatenate([xah[t], xah[t]], axis=0),
            preferred_element_type=F32,
        ) + jnp.dot(high, xal[t], preferred_element_type=F32)
        filter_ref[t] = out[0:128]
        yh, yl = halves(out[128:256])
        y_ref[t, 0:128, :] = yh
        y_ref[t, 128:256, :] = yl

    for d in range(1, 8):
        @pl.when(z + d <= 7)
        def _(copy=down_z[d]):
            copy.wait_recv()

    halves_swap = start(remote(cin.at[:, half_rows], cin.at[:, half_rows], other))
    halves_swap.wait_recv()
    c = [cin[d] for d in range(7)]
    upper = product(product(c[6], c[5]), product(c[4], c[3]))
    later = product(upper, product(product(c[2], c[1]), c[0]))
    later_ref[...] = jnp.where(odd, later, product(later, theirs))
    for d in range(1, 8):
        @pl.when(z >= d)
        def _(copy=down_z[d]):
            copy.wait_send()

    for copy in sent:
        copy.wait_send()


def smooth(later_ref, y_ref, filter_ref, smooth_out, filter_out, out, sem):
    f_out = pltpu.make_async_copy(filter_ref, filter_out, sem.at[8])
    out_t = [pltpu.make_async_copy(out.at[t], smooth_out.at[t], sem.at[t]) for t in range(8)]
    f_out.start()
    high, low = halves(later_ref[...])
    wide = jnp.concatenate([high, high], axis=1)
    for t in range(8):
        out[t] = jnp.dot(wide, y_ref[t], preferred_element_type=F32) + jnp.dot(
            low, y_ref[t, 0:128, :], preferred_element_type=F32
        )
        out_t[t].start()
    f_out.wait()
    for copy in out_t:
        copy.wait()


def local(prior, observations, spread, inflation, tiles, targets):
    anywhere = pl.BlockSpec(memory_space=pl.ANY)
    vmem = pl.BlockSpec(memory_space=pltpu.VMEM)
    whole = jax.ShapeDtypeStruct(prior.shape, F32)
    filtered, y, later = pl.pallas_call(
        assimilate,
        out_shape=(whole, jax.ShapeDtypeStruct((8, 256, 256), BF16), jax.ShapeDtypeStruct((128, 128), F32)),
        in_specs=[anywhere] * 6,
        out_specs=(vmem, vmem, vmem),
        scratch_shapes=[
            pltpu.VMEM((4, 4, 2, 128, 256), F32),
            pltpu.VMEM((4, 4096, 128), F32),
            pltpu.VMEM((2, 32, 256, 128), BF16),
            pltpu.VMEM((128, 256, 128), BF16),
            pltpu.VMEM((8, 128, 256), F32),
            pltpu.VMEM((8, 128, 256), BF16),
            pltpu.VMEM((8, 128, 256), BF16),
            pltpu.VMEM((4, 8, 512), F32),
            pltpu.VMEM((4, 4, 128), F32),
            pltpu.VMEM((4, 4, 8), jnp.int32),
            pltpu.SMEM((4, 4, 8), jnp.int32),
            pltpu.SMEM((8,), F32),
            pltpu.VMEM((2, 144, 256), F32),
            pltpu.VMEM((2, 136, 128), F32),
            pltpu.VMEM((4, 2, 136, 128), F32),
            pltpu.VMEM((8, 128, 128), F32),
            pltpu.VMEM((4, 128, 128), F32),
            pltpu.VMEM((128, 128), F32),
            pltpu.VMEM((128, 128), F32),
            pltpu.VMEM((128, 128), F32),
            pltpu.VMEM((7, 128, 128), F32),
            pltpu.VMEM((8, 128, 128), F32),
            pltpu.SemaphoreType.DMA((112,)),
            pltpu.SemaphoreType.DMA((112,)),
            pltpu.SemaphoreType.DMA((8,)),
        ],
        compiler_params=pltpu.CompilerParams(
            collective_id=0, has_side_effects=True, vmem_limit_bytes=VMEM_LIMIT
        ),
        name="assimilate",
    )(*[
        pltpu.with_memory_space_constraint(array, pltpu.HBM)
        for array in (prior, tiles.reshape(4096, 128), observations, spread.reshape(4, 128), targets, inflation)
    ])
    return pl.pallas_call(
        smooth,
        out_shape=(whole, whole),
        in_specs=[vmem, vmem, vmem],
        out_specs=(anywhere, anywhere),
        scratch_shapes=[
            pltpu.VMEM((8, 128, 256), F32),
            pltpu.SemaphoreType.DMA((9,)),
        ],
        compiler_params=pltpu.CompilerParams(vmem_limit_bytes=16 << 20),
        name="smooth",
    )(later, y, filtered)


def solution(mesh):
    placed = (
        P("tm", None, "row"),
        P("tm", "row"),
        P("row"),
        P("tm"),
        P("row", None, None, None),
        P("row", None),
    )
    return jax.shard_map(
        local,
        mesh=mesh,
        in_specs=placed,
        out_specs=(P("tm", None, "row"), P("tm", None, "row")),
        check_vma=False,
    )
```

```python
import functools

import jax
import jax.numpy as jnp
from jax import lax
from jax.experimental import pallas as pl
from jax.experimental.pallas import tpu as pltpu
from jax.sharding import PartitionSpec as P

MESH = pl.DeviceIdType.MESH
NS_ITERS = 8
VMEM_LIMIT = 40 << 20
F32, BF16 = jnp.float32, jnp.bfloat16
NT = (((1,), (1,)), ((), ()))


def halves(value):
    high = value.astype(BF16)
    low = (value - high.astype(F32)).astype(BF16)
    return high, low


def product(left, right):
    lh, ll = halves(left)
    rh, rl = halves(right)
    row = jnp.concatenate([rh, rl], axis=1)
    wide = jnp.dot(
        jnp.concatenate([lh, ll], axis=1),
        jnp.concatenate([row, row], axis=0),
        preferred_element_type=F32,
    )
    n = right.shape[1]
    return wide[:, :n] + wide[:, n:]


PIECE = 128
SHARED = 16 * PIECE
STEPS, BLOCK_ROWS = 2, 16


def assimilate(
    x_ref, tiles_ref, obs_ref, spread_ref, targets_ref, inflation_ref,
    filter_ref, y_ref, later_ref,
    xg, tg, xs, ts, xown, xah, xal, obg, spg, tgg, tgs, infl, acc, part, parts,
    u_ref, pbuf, pown, pother, cown, cin, rloc,
    send, recv, local_sem,
):
    tm, row = lax.axis_index("tm"), lax.axis_index("row")
    mx, my = lax.div(row, 4), lax.rem(row, 4)
    core = lax.rem(tm, 2)
    z = lax.div(tm, 2)
    other = (tm + 1 - 2 * core, row)
    counter = [0]

    def at(x, y):
        return (tm, lax.rem(x + 4, 4) * 4 + lax.rem(y + 4, 4))

    def along(d):
        return (lax.rem(tm + d + 16, 16), row)

    def remote(src, dst, device):
        i = counter[0]
        counter[0] += 1
        return pltpu.make_async_remote_copy(
            src_ref=src, dst_ref=dst, send_sem=send.at[i], recv_sem=recv.at[i],
            device_id=device, device_id_type=MESH,
        )

    own_x = lambda t: x_ref.at[2 * mx + t]
    own = [
        pltpu.make_async_copy(tiles_ref, tg.at[0], local_sem.at[0]),
        pltpu.make_async_copy(x_ref, xown, local_sem.at[1]),
        pltpu.make_async_copy(obs_ref, obg.at[0], local_sem.at[2]),
        pltpu.make_async_copy(spread_ref, spg.at[0], local_sem.at[3]),
        pltpu.make_async_copy(targets_ref, tgg.at[0], local_sem.at[4]),
        pltpu.make_async_copy(inflation_ref, infl, local_sem.at[5]),
        pltpu.make_async_copy(own_x(0), xg.at[0, 0, 0], local_sem.at[6]),
        pltpu.make_async_copy(own_x(1), xg.at[0, 0, 1], local_sem.at[7]),
    ]
    for copy in own:
        copy.start()

    eye = (
        lax.broadcasted_iota(jnp.int32, (128, 128), 0) == lax.broadcasted_iota(jnp.int32, (128, 128), 1)
    ).astype(F32)
    for d in range(7):
        cin[d] = eye
    barrier = pltpu.get_barrier_semaphore()
    near = [at(mx + d, my) for d in (1, 2, 3)] + [at(mx, my + d) for d in (1, 2, 3)]
    near += [other] + [along(2 * d) for d in range(1, 8)]
    for device in near:
        pl.semaphore_signal(barrier, inc=1, device_id=device, device_id_type=MESH)
    pl.semaphore_wait(barrier, len(near))

    sent = []

    def start(copy):
        copy.start()
        sent.append(copy)
        return copy

    across, up, down = {}, {}, {}

    def send_across(t):
        for d in (1, 3, 2):
            xd = lax.rem(mx + d, 4)
            across[t, d] = start(remote(x_ref.at[2 * xd + t], xg.at[d, 0, t], at(mx + d, my)))

    def send_y(t, k):
        src = own_x(t) if k == 0 else xg.at[k, 0, t]
        up[t, k] = start(remote(src, xg.at[k, 1, t], at(mx, my + 1)))
        down[t, k] = start(remote(src, xg.at[k, 3, t], at(mx, my - 1)))

    far = {}

    def pass_y(t, k):
        up[t, k].wait_recv()
        one = start(remote(xg.at[k, 1, t, 0:64], xg.at[k, 2, t, 0:64], at(mx, my + 1)))
        down[t, k].wait_recv()
        two = start(remote(xg.at[k, 3, t, 64:128], xg.at[k, 2, t, 64:128], at(mx, my - 1)))
        far[t, k] = (one, two)

    send_across(0)
    send_y(0, 0)
    send_y(1, 0)
    piece = pl.ds(PIECE * tm, PIECE)
    brought = [start(remote(tiles_ref.at[piece], tg.at[d, piece], at(mx + d, my))) for d in (1, 3, 2)]
    rest = (4096 - SHARED) // 4
    first = pl.ds(SHARED + 2 * rest * core, rest)
    second = pl.ds(SHARED + 2 * rest * core + rest, rest)

    send_across(1)
    passed = []

    def unit(step, low=0, size=PIECE):
        at_z = lax.rem(z + step + 8, 8)
        return tg.at[pl.ds(1, 3), pl.ds(PIECE * (2 * at_z + core) + low, size)]

    def send_z(step):
        if step < 4:
            ahead = start(remote(unit(1 - step), unit(1 - step), along(2)))
            behind = start(remote(unit(step - 1), unit(step - 1), along(-2)))
        else:
            half = PIECE // 2
            ahead = start(remote(unit(-3, 0, half), unit(-3, 0, half), along(2)))
            behind = start(remote(unit(3, half, half), unit(3, half, half), along(-2)))
        return ahead, behind

    def pass_on(ref):
        passed.append(start(remote(ref, ref, other)))

    def split_state(t, k, q):
        chunk = lax.rem(mx - k + 4, 4) * 4 + lax.rem(my - q + 4, 4)
        for half in (0, 1):
            high, low = halves(xg[k, q, t, :, half * 128:(half + 1) * 128])
            xs[t, 2 * chunk + half, 0:128, :] = high
            xs[t, 2 * chunk + half, 128:256, :] = low

    def split_tiles(k, low, high_end):
        @pl.loop(low, high_end)
        def _(n):
            high, low = halves(tg[k, pl.ds(pl.multiple_of(n * 128, 128), 128), :])
            ts[k * 32 + n, 0:128, :] = high
            ts[k * 32 + n, 128:256, :] = low

    def observe(t, k, rows=(0, 1, 2, 3)):
        lefts, rights = [], []
        for i in rows:
            index = [tgs[k, i, j] for j in range(8)]
            state = jnp.concatenate([xs[t, j] for j in index], axis=1)
            block = jnp.concatenate([ts[(k * 4 + i) * 8 + j] for j in range(8)], axis=1)
            wide = lax.dot_general(state, block, NT, preferred_element_type=F32)
            one = (wide[0:128, 0:128] + wide[0:128, 128:256]) + (wide[128:256, 0:128] + wide[128:256, 128:256])
            spread = spg[k, i:i + 1, :]
            mean = jnp.sum(one, axis=0, keepdims=True) * (1.0 / 128.0)
            wh, wl = halves((one - mean) * (spread * (127.0 ** -0.5)))
            seen = jnp.where(chosen[t], obg[k, :, i * 128:(i + 1) * 128], 0.0)
            innovation = (jnp.sum(seen, axis=0, keepdims=True) - mean) * spread
            ih, il = halves(jnp.broadcast_to(innovation, (16, 128)))
            upper = lax.broadcasted_iota(jnp.int32, (16, 128), 0) < 8
            lines = jnp.where(upper, ih.astype(F32), il.astype(F32)).astype(BF16)
            lefts.append(jnp.concatenate([wh, lines], axis=0))
            rights.append(jnp.concatenate([wh, wl], axis=0))
        acc[t] += lax.dot_general(
            jnp.concatenate(lefts, axis=1), jnp.concatenate(rights, axis=1), NT, preferred_element_type=F32
        )

    def reduce(t):
        cross = acc[t, 0:128, 128:256]
        part[t, 0:128, :] = acc[t, 0:128, 0:128] + cross + cross.T
        part[t, 128:136, :] = acc[t, 128:136, 0:128] + acc[t, 128:136, 128:256] + acc[t, 136:144, 0:128]
        return [start(remote(part.at[t], parts.at[d, t], at(mx, my + d))) for d in (1, 3, 2)]

    acc[...] = jnp.zeros_like(acc)
    chosen = [lax.broadcasted_iota(jnp.int32, (8, 128), 0) == 2 * mx + t for t in (0, 1)]
    across[0, 1].wait_recv()
    send_y(0, 1)
    across[0, 3].wait_recv()
    send_y(0, 3)
    across[0, 2].wait_recv()
    send_y(0, 2)
    right = [start(remote(tiles_ref.at[first], tg.at[1, first], at(mx + 1, my)))]
    left = [start(remote(tiles_ref.at[second], tg.at[3, second], at(mx - 1, my)))]
    pass_y(0, 0)
    pass_y(1, 0)
    for copy in brought:
        copy.wait_recv()
    steps = [send_z(1)]
    pass_on(unit(0))
    small = []
    for d in (1, 2, 3):
        small.append(start(remote(obs_ref, obg.at[d], at(mx + d, my))))
        small.append(start(remote(spread_ref, spg.at[d], at(mx + d, my))))
        small.append(start(remote(targets_ref, tgg.at[d], at(mx + d, my))))
    for copy in own:
        copy.wait()
    split_tiles(0, 0, 32)
    pass_y(0, 1)
    pass_y(0, 3)
    for copy in steps[0]:
        copy.wait_recv()
    steps.append(send_z(2))
    pass_on(unit(-1))
    pass_on(unit(1))
    for d in (1, 3, 2):
        across[1, d].wait_recv()
        send_y(1, d)
    right.append(start(remote(tiles_ref.at[second], tg.at[1, second], at(mx + 1, my))))
    left.append(start(remote(tiles_ref.at[first], tg.at[3, first], at(mx - 1, my))))
    pass_y(0, 2)
    right[0].wait_recv()
    right2 = start(remote(tg.at[1, first], tg.at[2, first], at(mx + 1, my)))
    left[0].wait_recv()
    left2 = start(remote(tg.at[3, second], tg.at[2, second], at(mx - 1, my)))
    for copy in small:
        copy.wait_recv()
    to_scalar = pltpu.make_async_copy(tgg, tgs, local_sem.at[0])
    to_scalar.start()
    for k in range(4):
        split_state(0, k, 0)
        split_state(0, k, 1)
        split_state(0, k, 3)
    pass_y(1, 1)
    for copy in steps[1]:
        copy.wait_recv()
    steps.append(send_z(3))
    pass_on(unit(-2))
    pass_on(unit(2))
    for k in (0, 1, 3, 2):
        for copy in far[0, k]:
            copy.wait_recv()
        split_state(0, k, 2)
        split_state(1, k, 0)
    right[1].wait_recv()
    pass_on(tg.at[1, pl.ds(SHARED + 2 * rest * core, 2 * rest)])
    left[1].wait_recv()
    pass_on(tg.at[3, pl.ds(SHARED + 2 * rest * core, 2 * rest)])
    pass_y(1, 3)
    to_scalar.wait()
    observe(0, 0, (0, 1))
    pass_y(1, 2)
    for copy in steps[2]:
        copy.wait_recv()
    steps.append(send_z(4))
    pass_on(unit(-3))
    pass_on(unit(3))
    right2.wait_recv()
    left2.wait_recv()
    pass_on(tg.at[2, pl.ds(SHARED + 2 * rest * core, 2 * rest)])
    observe(0, 0, (2, 3))
    for t in range(8):
        xah[t], xal[t] = halves(xown[t])
    for k in range(4):
        split_state(1, k, 1)
        split_state(1, k, 3)
    passed[5].wait_recv()
    passed[6].wait_recv()
    passed[9].wait_recv()
    shared_tiles = SHARED // 128
    shared_rows, direct_rows = range(SHARED // 1024), range(SHARED // 1024, 4)
    for k in (1, 3):
        split_tiles(k, shared_tiles, 32)
        observe(0, k, direct_rows)
    for copy in steps[3]:
        copy.wait_recv()
    pass_on(unit(4))
    split_tiles(2, shared_tiles, 32)
    observe(0, 2, direct_rows)
    for i, copy in enumerate(passed):
        if i not in (5, 6, 9):
            copy.wait_recv()
    for k in (1, 2, 3):
        split_tiles(k, 0, shared_tiles)
        observe(0, k, shared_rows)
    sums = reduce(0)
    for k in (0, 1, 3, 2):
        for copy in far[1, k]:
            copy.wait_recv()
    for k in range(4):
        split_state(1, k, 2)
    for k in range(4):
        observe(1, k)
    sums += reduce(1)
    for copy in sums:
        copy.wait_recv()

    state = []
    for t in (0, 1):
        total = part[t] + parts[1, t] + parts[2, t] + parts[3, t]
        info = total[0:128, :] + eye
        bound = jnp.max(jnp.sum(jnp.abs(info), axis=0, keepdims=True), axis=1, keepdims=True)
        m = info / bound
        state.append([m, 1.5 * eye - 0.5 * m, bound, total[128:136, :]])
    for _ in range(NS_ITERS - 1):
        for s in state:
            square = product(s[0], s[0])
            s[0] = product(s[0], 2.25 * eye - 1.5 * s[0] + 0.25 * square)
            s[1] = product(1.5 * eye - 0.5 * s[0], s[1])
    for t, (_, q, bound, vector) in enumerate(state):
        root = q / jnp.sqrt(bound)
        weights = product(product(vector, root), root)[0:1, :]
        mixing = weights * (127.0 ** -0.5) + infl[2 * mx + t] * root
        mixing = mixing - jnp.sum(mixing, axis=1, keepdims=True) * (1.0 / 128.0) + 1.0 / 128.0
        u_ref[2 * mx + t] = mixing
    pbuf[mx] = product(u_ref[2 * mx + 1], u_ref[2 * mx])
    pairs = [start(remote(pbuf.at[mx], pbuf.at[mx], at(mx + d, my))) for d in (1, 3, 2)]
    for copy in pairs:
        copy.wait_recv()
    mine = u_ref.at[pl.ds(2 * mx, 2)]
    shared = [start(remote(mine, mine, at(mx + d, my))) for d in (1, 3, 2)]

    p0, p1, p2, p3 = [pbuf[i] for i in range(4)]
    p23 = product(p3, p2)
    p03 = product(p23, product(p1, p0))
    pown[...] = p03
    swap = start(remote(pown, pother, other))
    rloc[0] = p03
    rloc[4] = p23
    rloc[6] = p3
    swap.wait_recv()
    theirs = pother[...]
    odd = core == 1
    cown[...] = product(jnp.where(odd, p03, theirs), jnp.where(odd, theirs, p03))
    half_rows = pl.ds(64 * core, 64)
    down_z = {}
    for d in (4, 3, 5, 2, 6, 1, 7):
        copy = remote(cown.at[half_rows], cin.at[d - 1, half_rows], along(-2 * d))
        down_z[d] = copy

        @pl.when(z >= d)
        def _(copy=copy):
            copy.start()

    for copy in shared:
        copy.wait_recv()
    r2 = product(p23, p1)
    rloc[2] = r2
    rloc[7] = u_ref[7]
    rloc[5] = product(p3, u_ref[5])
    rloc[3] = product(p23, u_ref[3])
    rloc[1] = product(r2, u_ref[1])
    for t in range(8):
        both = jnp.concatenate([u_ref[t], rloc[t]], axis=0)
        high, low = halves(both)
        out = jnp.dot(
            jnp.concatenate([high, low], axis=1), jnp.concatenate([xah[t], xah[t]], axis=0),
            preferred_element_type=F32,
        ) + jnp.dot(high, xal[t], preferred_element_type=F32)
        filter_ref[t] = out[0:128]
        yh, yl = halves(out[128:256])
        y_ref[t, 0:128, :] = yh
        y_ref[t, 128:256, :] = yl

    for copy in sent:
        copy.wait_send()
    sent.clear()
    for d in range(1, 8):
        @pl.when(z + d <= 7)
        def _(copy=down_z[d]):
            copy.wait_recv()

    halves_swap = start(remote(cin.at[:, half_rows], cin.at[:, half_rows], other))
    halves_swap.wait_recv()
    c = [cin[d] for d in range(7)]
    upper = product(product(c[6], c[5]), product(c[4], c[3]))
    later = product(upper, product(product(c[2], c[1]), c[0]))
    later_ref[...] = jnp.where(odd, later, product(later, theirs))
    for d in range(1, 8):
        @pl.when(z >= d)
        def _(copy=down_z[d]):
            copy.wait_send()

    for copy in sent:
        copy.wait_send()


def smooth(later_ref, y_ref, filter_ref, smooth_out, filter_out, out, sem):
    f_out = pltpu.make_async_copy(filter_ref, filter_out, sem.at[8])
    out_t = [pltpu.make_async_copy(out.at[t], smooth_out.at[t], sem.at[t]) for t in range(8)]
    f_out.start()
    high, low = halves(later_ref[...])
    wide = jnp.concatenate([high, high], axis=1)
    for t in range(8):
        out[t] = jnp.dot(wide, y_ref[t], preferred_element_type=F32) + jnp.dot(
            low, y_ref[t, 0:128, :], preferred_element_type=F32
        )
        out_t[t].start()
    f_out.wait()
    for copy in out_t:
        copy.wait()


def local(prior, observations, spread, inflation, tiles, targets):
    anywhere = pl.BlockSpec(memory_space=pl.ANY)
    vmem = pl.BlockSpec(memory_space=pltpu.VMEM)
    whole = jax.ShapeDtypeStruct(prior.shape, F32)
    filtered, y, later = pl.pallas_call(
        assimilate,
        out_shape=(whole, jax.ShapeDtypeStruct((8, 256, 256), BF16), jax.ShapeDtypeStruct((128, 128), F32)),
        in_specs=[anywhere] * 6,
        out_specs=(vmem, vmem, vmem),
        scratch_shapes=[
            pltpu.VMEM((4, 4, 2, 128, 256), F32),
            pltpu.VMEM((4, 4096, 128), F32),
            pltpu.VMEM((2, 32, 256, 128), BF16),
            pltpu.VMEM((128, 256, 128), BF16),
            pltpu.VMEM((8, 128, 256), F32),
            pltpu.VMEM((8, 128, 256), BF16),
            pltpu.VMEM((8, 128, 256), BF16),
            pltpu.VMEM((4, 8, 512), F32),
            pltpu.VMEM((4, 4, 128), F32),
            pltpu.VMEM((4, 4, 8), jnp.int32),
            pltpu.SMEM((4, 4, 8), jnp.int32),
            pltpu.SMEM((8,), F32),
            pltpu.VMEM((2, 144, 256), F32),
            pltpu.VMEM((2, 136, 128), F32),
            pltpu.VMEM((4, 2, 136, 128), F32),
            pltpu.VMEM((8, 128, 128), F32),
            pltpu.VMEM((4, 128, 128), F32),
            pltpu.VMEM((128, 128), F32),
            pltpu.VMEM((128, 128), F32),
            pltpu.VMEM((128, 128), F32),
            pltpu.VMEM((7, 128, 128), F32),
            pltpu.VMEM((8, 128, 128), F32),
            pltpu.SemaphoreType.DMA((112,)),
            pltpu.SemaphoreType.DMA((112,)),
            pltpu.SemaphoreType.DMA((8,)),
        ],
        compiler_params=pltpu.CompilerParams(
            collective_id=0, has_side_effects=True, vmem_limit_bytes=VMEM_LIMIT
        ),
        name="assimilate",
    )(*[
        pltpu.with_memory_space_constraint(array, pltpu.HBM)
        for array in (prior, tiles.reshape(4096, 128), observations, spread.reshape(4, 128), targets, inflation)
    ])
    return pl.pallas_call(
        smooth,
        out_shape=(whole, whole),
        in_specs=[vmem, vmem, vmem],
        out_specs=(anywhere, anywhere),
        scratch_shapes=[
            pltpu.VMEM((8, 128, 256), F32),
            pltpu.SemaphoreType.DMA((9,)),
        ],
        compiler_params=pltpu.CompilerParams(vmem_limit_bytes=16 << 20),
        name="smooth",
    )(later, y, filtered)


def solution(mesh):
    placed = (
        P("tm", None, "row"),
        P("tm", "row"),
        P("row"),
        P("tm"),
        P("row", None, None, None),
        P("row", None),
    )
    return jax.shard_map(
        local,
        mesh=mesh,
        in_specs=placed,
        out_specs=(P("tm", None, "row"), P("tm", None, "row")),
        check_vma=False,
    )
```

```python
import functools

import jax
import jax.numpy as jnp
from jax import lax
from jax.experimental import pallas as pl
from jax.experimental.pallas import tpu as pltpu
from jax.sharding import PartitionSpec as P

MESH = pl.DeviceIdType.MESH
NS_ITERS = 8
VMEM_LIMIT = 40 << 20
F32, BF16 = jnp.float32, jnp.bfloat16
NT = (((1,), (1,)), ((), ()))


def halves(value):
    high = value.astype(BF16)
    low = (value - high.astype(F32)).astype(BF16)
    return high, low


def product(left, right):
    lh, ll = halves(left)
    rh, rl = halves(right)
    row = jnp.concatenate([rh, rl], axis=1)
    wide = jnp.dot(
        jnp.concatenate([lh, ll], axis=1),
        jnp.concatenate([row, row], axis=0),
        preferred_element_type=F32,
    )
    n = right.shape[1]
    return wide[:, :n] + wide[:, n:]


PIECE = 128
SHARED = 16 * PIECE
STEPS, BLOCK_ROWS = 2, 16


def assimilate(
    x_ref, tiles_ref, obs_ref, spread_ref, targets_ref, inflation_ref,
    filter_ref, y_ref, later_ref,
    xg, tg, xs, ts, xown, xah, xal, obg, spg, tgg, tgs, infl, acc, part, parts,
    u_ref, pbuf, pown, pother, cown, cin, rloc,
    send, recv, local_sem,
):
    tm, row = lax.axis_index("tm"), lax.axis_index("row")
    mx, my = lax.div(row, 4), lax.rem(row, 4)
    core = lax.rem(tm, 2)
    z = lax.div(tm, 2)
    other = (tm + 1 - 2 * core, row)
    counter = [0]

    def at(x, y):
        return (tm, lax.rem(x + 4, 4) * 4 + lax.rem(y + 4, 4))

    def along(d):
        return (lax.rem(tm + d + 16, 16), row)

    def remote(src, dst, device):
        i = counter[0]
        counter[0] += 1
        return pltpu.make_async_remote_copy(
            src_ref=src, dst_ref=dst, send_sem=send.at[i], recv_sem=recv.at[i],
            device_id=device, device_id_type=MESH,
        )

    own_x = lambda t: x_ref.at[2 * mx + t]
    own = [
        pltpu.make_async_copy(tiles_ref, tg.at[0], local_sem.at[0]),
        pltpu.make_async_copy(x_ref, xown, local_sem.at[1]),
        pltpu.make_async_copy(obs_ref, obg.at[0], local_sem.at[2]),
        pltpu.make_async_copy(spread_ref, spg.at[0], local_sem.at[3]),
        pltpu.make_async_copy(targets_ref, tgg.at[0], local_sem.at[4]),
        pltpu.make_async_copy(inflation_ref, infl, local_sem.at[5]),
        pltpu.make_async_copy(own_x(0), xg.at[0, 0, 0], local_sem.at[6]),
        pltpu.make_async_copy(own_x(1), xg.at[0, 0, 1], local_sem.at[7]),
    ]
    for copy in own:
        copy.start()

    eye = (
        lax.broadcasted_iota(jnp.int32, (128, 128), 0) == lax.broadcasted_iota(jnp.int32, (128, 128), 1)
    ).astype(F32)
    for d in range(7):
        cin[d] = eye
    barrier = pltpu.get_barrier_semaphore()
    near = [at(mx + d, my) for d in (1, 2, 3)] + [at(mx, my + d) for d in (1, 2, 3)]
    near += [other] + [along(2 * d) for d in range(1, 8)]
    for device in near:
        pl.semaphore_signal(barrier, inc=1, device_id=device, device_id_type=MESH)
    pl.semaphore_wait(barrier, len(near))

    sent = []

    def start(copy):
        copy.start()
        sent.append(copy)
        return copy

    across, up, down = {}, {}, {}

    def send_across(t):
        for d in (1, 3, 2):
            xd = lax.rem(mx + d, 4)
            across[t, d] = start(remote(x_ref.at[2 * xd + t], xg.at[d, 0, t], at(mx + d, my)))

    def send_y(t, k):
        src = own_x(t) if k == 0 else xg.at[k, 0, t]
        up[t, k] = start(remote(src, xg.at[k, 1, t], at(mx, my + 1)))
        down[t, k] = start(remote(src, xg.at[k, 3, t], at(mx, my - 1)))

    far = {}

    def pass_y(t, k):
        up[t, k].wait_recv()
        one = start(remote(xg.at[k, 1, t, 0:64], xg.at[k, 2, t, 0:64], at(mx, my + 1)))
        down[t, k].wait_recv()
        two = start(remote(xg.at[k, 3, t, 64:128], xg.at[k, 2, t, 64:128], at(mx, my - 1)))
        far[t, k] = (one, two)

    send_across(0)
    send_y(0, 0)
    send_y(1, 0)
    piece = pl.ds(PIECE * tm, PIECE)
    brought = [start(remote(tiles_ref.at[piece], tg.at[d, piece], at(mx + d, my))) for d in (1, 3, 2)]
    rest = (4096 - SHARED) // 4
    first = pl.ds(SHARED + 2 * rest * core, rest)
    second = pl.ds(SHARED + 2 * rest * core + rest, rest)

    send_across(1)
    passed = []

    def unit(step, low=0, size=PIECE):
        at_z = lax.rem(z + step + 8, 8)
        return tg.at[pl.ds(1, 3), pl.ds(PIECE * (2 * at_z + core) + low, size)]

    def send_z(step):
        if step < 4:
            ahead = start(remote(unit(1 - step), unit(1 - step), along(2)))
            behind = start(remote(unit(step - 1), unit(step - 1), along(-2)))
        else:
            half = PIECE // 2
            ahead = start(remote(unit(-3, 0, half), unit(-3, 0, half), along(2)))
            behind = start(remote(unit(3, half, half), unit(3, half, half), along(-2)))
        return ahead, behind

    def pass_on(ref):
        passed.append(start(remote(ref, ref, other)))

    def split_state(t, k, q):
        chunk = lax.rem(mx - k + 4, 4) * 4 + lax.rem(my - q + 4, 4)
        for half in (0, 1):
            high, low = halves(xg[k, q, t, :, half * 128:(half + 1) * 128])
            xs[t, 2 * chunk + half, 0:128, :] = high
            xs[t, 2 * chunk + half, 128:256, :] = low

    def split_tiles(k, low, high_end):
        @pl.loop(low, high_end)
        def _(n):
            high, low = halves(tg[k, pl.ds(pl.multiple_of(n * 128, 128), 128), :])
            ts[k * 32 + n, 0:128, :] = high
            ts[k * 32 + n, 128:256, :] = low

    def observe(t, blocks, rows=(0, 1, 2, 3)):
        lefts, rights = [], []
        for k, i in [(k, i) for k in blocks for i in rows]:
            index = [tgs[k, i, j] for j in range(8)]
            state = jnp.concatenate([xs[t, j] for j in index], axis=1)
            block = jnp.concatenate([ts[(k * 4 + i) * 8 + j] for j in range(8)], axis=1)
            wide = lax.dot_general(state, block, NT, preferred_element_type=F32)
            one = (wide[0:128, 0:128] + wide[0:128, 128:256]) + (wide[128:256, 0:128] + wide[128:256, 128:256])
            spread = spg[k, i:i + 1, :]
            mean = jnp.sum(one, axis=0, keepdims=True) * (1.0 / 128.0)
            wh, wl = halves((one - mean) * (spread * (127.0 ** -0.5)))
            seen = jnp.where(chosen[t], obg[k, :, i * 128:(i + 1) * 128], 0.0)
            innovation = (jnp.sum(seen, axis=0, keepdims=True) - mean) * spread
            ih, il = halves(jnp.broadcast_to(innovation, (16, 128)))
            upper = lax.broadcasted_iota(jnp.int32, (16, 128), 0) < 8
            lines = jnp.where(upper, ih.astype(F32), il.astype(F32)).astype(BF16)
            lefts.append(jnp.concatenate([wh, lines], axis=0))
            rights.append(jnp.concatenate([wh, wl], axis=0))
        acc[t] += lax.dot_general(
            jnp.concatenate(lefts, axis=1), jnp.concatenate(rights, axis=1), NT, preferred_element_type=F32
        )

    def reduce(t):
        cross = acc[t, 0:128, 128:256]
        part[t, 0:128, :] = acc[t, 0:128, 0:128] + cross + cross.T
        part[t, 128:136, :] = acc[t, 128:136, 0:128] + acc[t, 128:136, 128:256] + acc[t, 136:144, 0:128]
        return [start(remote(part.at[t], parts.at[d, t], at(mx, my + d))) for d in (1, 3, 2)]

    acc[...] = jnp.zeros_like(acc)
    chosen = [lax.broadcasted_iota(jnp.int32, (8, 128), 0) == 2 * mx + t for t in (0, 1)]
    across[0, 1].wait_recv()
    send_y(0, 1)
    across[0, 3].wait_recv()
    send_y(0, 3)
    across[0, 2].wait_recv()
    send_y(0, 2)
    right = [start(remote(tiles_ref.at[first], tg.at[1, first], at(mx + 1, my)))]
    left = [start(remote(tiles_ref.at[second], tg.at[3, second], at(mx - 1, my)))]
    pass_y(0, 0)
    pass_y(1, 0)
    for copy in brought:
        copy.wait_recv()
    steps = [send_z(1)]
    pass_on(unit(0))
    small = []
    for d in (1, 2, 3):
        small.append(start(remote(obs_ref, obg.at[d], at(mx + d, my))))
        small.append(start(remote(spread_ref, spg.at[d], at(mx + d, my))))
        small.append(start(remote(targets_ref, tgg.at[d], at(mx + d, my))))
    for copy in own:
        copy.wait()
    split_tiles(0, 0, 32)
    pass_y(0, 1)
    pass_y(0, 3)
    for copy in steps[0]:
        copy.wait_recv()
    steps.append(send_z(2))
    pass_on(unit(-1))
    pass_on(unit(1))
    for d in (1, 3, 2):
        across[1, d].wait_recv()
        send_y(1, d)
    right.append(start(remote(tiles_ref.at[second], tg.at[1, second], at(mx + 1, my))))
    left.append(start(remote(tiles_ref.at[first], tg.at[3, first], at(mx - 1, my))))
    pass_y(0, 2)
    right[0].wait_recv()
    right2 = start(remote(tg.at[1, first], tg.at[2, first], at(mx + 1, my)))
    left[0].wait_recv()
    left2 = start(remote(tg.at[3, second], tg.at[2, second], at(mx - 1, my)))
    for copy in small:
        copy.wait_recv()
    to_scalar = pltpu.make_async_copy(tgg, tgs, local_sem.at[0])
    to_scalar.start()
    for k in range(4):
        split_state(0, k, 0)
        split_state(0, k, 1)
        split_state(0, k, 3)
    pass_y(1, 1)
    for copy in steps[1]:
        copy.wait_recv()
    steps.append(send_z(3))
    pass_on(unit(-2))
    pass_on(unit(2))
    for k in (0, 1, 3, 2):
        for copy in far[0, k]:
            copy.wait_recv()
        split_state(0, k, 2)
        split_state(1, k, 0)
    right[1].wait_recv()
    pass_on(tg.at[1, pl.ds(SHARED + 2 * rest * core, 2 * rest)])
    left[1].wait_recv()
    pass_on(tg.at[3, pl.ds(SHARED + 2 * rest * core, 2 * rest)])
    pass_y(1, 3)
    to_scalar.wait()
    observe(0, (0,), (0, 1))
    pass_y(1, 2)
    for copy in steps[2]:
        copy.wait_recv()
    steps.append(send_z(4))
    pass_on(unit(-3))
    pass_on(unit(3))
    right2.wait_recv()
    left2.wait_recv()
    pass_on(tg.at[2, pl.ds(SHARED + 2 * rest * core, 2 * rest)])
    observe(0, (0,), (2, 3))
    for t in range(8):
        xah[t], xal[t] = halves(xown[t])
    for k in range(4):
        split_state(1, k, 1)
        split_state(1, k, 3)
    passed[5].wait_recv()
    passed[6].wait_recv()
    passed[9].wait_recv()
    shared_tiles = SHARED // 128
    shared_rows, direct_rows = range(SHARED // 1024), range(SHARED // 1024, 4)
    for k in (1, 3):
        split_tiles(k, shared_tiles, 32)
        observe(0, (k,), direct_rows)
    for copy in steps[3]:
        copy.wait_recv()
    pass_on(unit(4))
    split_tiles(2, shared_tiles, 32)
    observe(0, (2,), direct_rows)
    for i, copy in enumerate(passed):
        if i not in (5, 6, 9):
            copy.wait_recv()
    for k in (1, 2, 3):
        split_tiles(k, 0, shared_tiles)
    observe(0, (1, 2, 3), shared_rows)
    sums = reduce(0)
    for k in (0, 1, 3, 2):
        for copy in far[1, k]:
            copy.wait_recv()
    for k in range(4):
        split_state(1, k, 2)
    observe(1, range(4))
    sums += reduce(1)
    for copy in sums:
        copy.wait_recv()

    state = []
    for t in (0, 1):
        total = part[t] + parts[1, t] + parts[2, t] + parts[3, t]
        info = total[0:128, :] + eye
        bound = jnp.max(jnp.sum(jnp.abs(info), axis=0, keepdims=True), axis=1, keepdims=True)
        m = info / bound
        state.append([m, 1.5 * eye - 0.5 * m, bound, total[128:136, :]])
    for _ in range(NS_ITERS - 1):
        for s in state:
            square = product(s[0], s[0])
            s[0] = product(s[0], 2.25 * eye - 1.5 * s[0] + 0.25 * square)
            s[1] = product(1.5 * eye - 0.5 * s[0], s[1])
    for t, (_, q, bound, vector) in enumerate(state):
        root = q / jnp.sqrt(bound)
        weights = product(product(vector, root), root)[0:1, :]
        mixing = weights * (127.0 ** -0.5) + infl[2 * mx + t] * root
        mixing = mixing - jnp.sum(mixing, axis=1, keepdims=True) * (1.0 / 128.0) + 1.0 / 128.0
        u_ref[2 * mx + t] = mixing
    pbuf[mx] = product(u_ref[2 * mx + 1], u_ref[2 * mx])
    pairs = [start(remote(pbuf.at[mx], pbuf.at[mx], at(mx + d, my))) for d in (1, 3, 2)]
    for copy in pairs:
        copy.wait_recv()
    mine = u_ref.at[pl.ds(2 * mx, 2)]
    shared = [start(remote(mine, mine, at(mx + d, my))) for d in (1, 3, 2)]

    p0, p1, p2, p3 = [pbuf[i] for i in range(4)]
    p23 = product(p3, p2)
    p03 = product(p23, product(p1, p0))
    pown[...] = p03
    swap = start(remote(pown, pother, other))
    rloc[0] = p03
    rloc[4] = p23
    rloc[6] = p3
    swap.wait_recv()
    theirs = pother[...]
    odd = core == 1
    cown[...] = product(jnp.where(odd, p03, theirs), jnp.where(odd, theirs, p03))
    half_rows = pl.ds(64 * core, 64)
    down_z = {}
    for d in (4, 3, 5, 2, 6, 1, 7):
        copy = remote(cown.at[half_rows], cin.at[d - 1, half_rows], along(-2 * d))
        down_z[d] = copy

        @pl.when(z >= d)
        def _(copy=copy):
            copy.start()

    for copy in shared:
        copy.wait_recv()
    r2 = product(p23, p1)
    rloc[2] = r2
    rloc[7] = u_ref[7]
    rloc[5] = product(p3, u_ref[5])
    rloc[3] = product(p23, u_ref[3])
    rloc[1] = product(r2, u_ref[1])
    for t in range(8):
        both = jnp.concatenate([u_ref[t], rloc[t]], axis=0)
        high, low = halves(both)
        out = jnp.dot(
            jnp.concatenate([high, low], axis=1), jnp.concatenate([xah[t], xah[t]], axis=0),
            preferred_element_type=F32,
        ) + jnp.dot(high, xal[t], preferred_element_type=F32)
        filter_ref[t] = out[0:128]
        yh, yl = halves(out[128:256])
        y_ref[t, 0:128, :] = yh
        y_ref[t, 128:256, :] = yl

    for copy in sent:
        copy.wait_send()
    sent.clear()
    for d in range(1, 8):
        @pl.when(z + d <= 7)
        def _(copy=down_z[d]):
            copy.wait_recv()

    halves_swap = start(remote(cin.at[:, half_rows], cin.at[:, half_rows], other))
    halves_swap.wait_recv()
    c = [cin[d] for d in range(7)]
    upper = product(product(c[6], c[5]), product(c[4], c[3]))
    later = product(upper, product(product(c[2], c[1]), c[0]))
    later_ref[...] = jnp.where(odd, later, product(later, theirs))
    for d in range(1, 8):
        @pl.when(z >= d)
        def _(copy=down_z[d]):
            copy.wait_send()

    for copy in sent:
        copy.wait_send()


def smooth(later_ref, y_ref, filter_ref, smooth_out, filter_out, out, sem):
    f_out = pltpu.make_async_copy(filter_ref, filter_out, sem.at[8])
    out_t = [pltpu.make_async_copy(out.at[t], smooth_out.at[t], sem.at[t]) for t in range(8)]
    f_out.start()
    high, low = halves(later_ref[...])
    wide = jnp.concatenate([high, high], axis=1)
    for t in range(8):
        out[t] = jnp.dot(wide, y_ref[t], preferred_element_type=F32) + jnp.dot(
            low, y_ref[t, 0:128, :], preferred_element_type=F32
        )
        out_t[t].start()
    f_out.wait()
    for copy in out_t:
        copy.wait()


def local(prior, observations, spread, inflation, tiles, targets):
    anywhere = pl.BlockSpec(memory_space=pl.ANY)
    vmem = pl.BlockSpec(memory_space=pltpu.VMEM)
    whole = jax.ShapeDtypeStruct(prior.shape, F32)
    filtered, y, later = pl.pallas_call(
        assimilate,
        out_shape=(whole, jax.ShapeDtypeStruct((8, 256, 256), BF16), jax.ShapeDtypeStruct((128, 128), F32)),
        in_specs=[anywhere] * 6,
        out_specs=(vmem, vmem, vmem),
        scratch_shapes=[
            pltpu.VMEM((4, 4, 2, 128, 256), F32),
            pltpu.VMEM((4, 4096, 128), F32),
            pltpu.VMEM((2, 32, 256, 128), BF16),
            pltpu.VMEM((128, 256, 128), BF16),
            pltpu.VMEM((8, 128, 256), F32),
            pltpu.VMEM((8, 128, 256), BF16),
            pltpu.VMEM((8, 128, 256), BF16),
            pltpu.VMEM((4, 8, 512), F32),
            pltpu.VMEM((4, 4, 128), F32),
            pltpu.VMEM((4, 4, 8), jnp.int32),
            pltpu.SMEM((4, 4, 8), jnp.int32),
            pltpu.SMEM((8,), F32),
            pltpu.VMEM((2, 144, 256), F32),
            pltpu.VMEM((2, 136, 128), F32),
            pltpu.VMEM((4, 2, 136, 128), F32),
            pltpu.VMEM((8, 128, 128), F32),
            pltpu.VMEM((4, 128, 128), F32),
            pltpu.VMEM((128, 128), F32),
            pltpu.VMEM((128, 128), F32),
            pltpu.VMEM((128, 128), F32),
            pltpu.VMEM((7, 128, 128), F32),
            pltpu.VMEM((8, 128, 128), F32),
            pltpu.SemaphoreType.DMA((112,)),
            pltpu.SemaphoreType.DMA((112,)),
            pltpu.SemaphoreType.DMA((8,)),
        ],
        compiler_params=pltpu.CompilerParams(
            collective_id=0, has_side_effects=True, vmem_limit_bytes=VMEM_LIMIT
        ),
        name="assimilate",
    )(*[
        pltpu.with_memory_space_constraint(array, pltpu.HBM)
        for array in (prior, tiles.reshape(4096, 128), observations, spread.reshape(4, 128), targets, inflation)
    ])
    return pl.pallas_call(
        smooth,
        out_shape=(whole, whole),
        in_specs=[vmem, vmem, vmem],
        out_specs=(anywhere, anywhere),
        scratch_shapes=[
            pltpu.VMEM((8, 128, 256), F32),
            pltpu.SemaphoreType.DMA((9,)),
        ],
        compiler_params=pltpu.CompilerParams(vmem_limit_bytes=16 << 20),
        name="smooth",
    )(later, y, filtered)


def solution(mesh):
    placed = (
        P("tm", None, "row"),
        P("tm", "row"),
        P("row"),
        P("tm"),
        P("row", None, None, None),
        P("row", None),
    )
    return jax.shard_map(
        local,
        mesh=mesh,
        in_specs=placed,
        out_specs=(P("tm", None, "row"), P("tm", None, "row")),
        check_vma=False,
    )
```
